128 devices in a mesh: samp: 16 (over z_hi, x, core), par: 8 (over y, z_lo).
Axes of the slice: x: 4, y: 4, z: 4 (z_hi: 2, z_lo: 2; z = z_hi * 2 + z_lo), core: 2. Of those that a mesh axis runs over, the one named last changes fastest.
Arguments:
- activations: bfloat16 [10240, 2048], P('samp', 'par'), may hold values from -128 to 128
- signal: bfloat16 [10240, 2], P('samp'), may hold values from -40 to 40
Outputs:
- gram: float32 [10240, 10240], P('samp', 'par')
- panels: float32 [10240, 1280], P('samp', 'par')
The draws below stay inside these ranges and needn't reach their ends.
All inputs are finite; a program needn't handle non-finite values.
Results may differ from the reference program's by a relative error of at most 0.0022.
Values may be sent and summed in bfloat16 or wider, within the bound.
A program may use at most 128 MiB of HBM per device.

```python
import jax
import jax.numpy as jnp
from jax import lax

HID = 2048
OUT = 2
SLAB = 4096
SAMPLES = 10240
PW = 640


def joint_latent(key):
    return jax.random.uniform(jax.random.fold_in(key, 21), (SAMPLES, 1), minval=-0.8, maxval=0.8)


def draw_activations(key, part):
    latent = joint_latent(key)
    coupling = jax.random.uniform(jax.random.fold_in(key, 22), (1, HID), minval=-1.0, maxval=1.0)
    centers = jax.random.uniform(jax.random.fold_in(key, 23), (1, HID), minval=-0.8, maxval=0.8)
    column_size = jnp.exp(jax.random.uniform(jax.random.fold_in(key, 24), (1, HID), minval=0.0, maxval=jnp.log(10.0)))
    noise = jax.random.normal(jax.random.fold_in(key, 25), (SAMPLES, HID))
    values = centers + noise
    values = values * column_size * jnp.exp(coupling * latent)
    return jnp.clip(values, -128.0, 128.0).astype(jnp.bfloat16)


def draw_signal(key, part):
    latent = joint_latent(key)
    rising = 1.0 + 2.0 * jnp.arange(SAMPLES, dtype=jnp.float32)[:, None] / (SAMPLES - 1)
    means = jax.random.uniform(jax.random.fold_in(key, 31), (1, OUT), minval=0.4, maxval=0.9)
    direction = jnp.where(jnp.arange(OUT) % 2 == 0, 1.0, -1.0).astype(jnp.float32)[None, :]
    noise = jax.random.normal(jax.random.fold_in(key, 32), (SAMPLES, OUT))
    values = (means + noise) * rising * jnp.exp(latent * direction)
    return jnp.clip(values, -40.0, 40.0).astype(jnp.bfloat16)


def setup_inputs(seed: int = 0) -> dict:
    key_of = jax.random.split(jax.random.key(seed), 3)
    activations = draw_activations(jax.random.fold_in(key_of[2], 71), 0)
    signal = draw_signal(jax.random.fold_in(key_of[2], 71), 0)
    return dict(activations=activations, signal=signal)


DAMPING = 0.5
EPSILON = 1e-05

def right_solve(factor, block):
    return jax.scipy.linalg.solve_triangular(factor, block.T, lower=True).T

def reference(activations, signal):
    signal_float = signal.astype(jnp.float32)
    active_float = activations.astype(jnp.float32)
    average = jnp.dot(signal.T.astype(jnp.float32), activations.astype(jnp.float32), preferred_element_type=jnp.float32) / SAMPLES
    products = signal_float[:, :, None] * active_float[:, None, :]
    second = lax.optimization_barrier(jnp.sum(products * products, axis=0)) / SAMPLES
    column_scale = 1.0 / jnp.sqrt(SLAB * (second - average * average + EPSILON))
    centered = products - average[None]
    jacobian = (centered * column_scale[None]).reshape(SAMPLES, SLAB).astype(jnp.bfloat16)
    gram = jnp.dot(jacobian.astype(jnp.float32), jacobian.T.astype(jnp.float32), preferred_element_type=jnp.float32)
    gram = gram + DAMPING * jnp.eye(SAMPLES, dtype=jnp.float32)
    factor_one = jnp.linalg.cholesky(gram[:PW, :PW])
    panel_one = right_solve(factor_one, gram[:, :PW])
    update = gram[:, PW:2 * PW] - jnp.dot(panel_one, panel_one[PW:2 * PW].T, precision=lax.Precision.HIGHEST)
    factor_two = jnp.linalg.cholesky(update[PW:2 * PW])
    panel_two = right_solve(factor_two, update)
    row_index = lax.broadcasted_iota(jnp.int32, panel_two.shape, 0)
    panel_two = jnp.where(row_index < PW, jnp.float32(0.0), panel_two)
    return (gram, jnp.concatenate([panel_one, panel_two], axis=1))
```

```python
import functools

import jax
import jax.numpy as jnp
from jax import lax
from jax.experimental import pallas as pl
from jax.experimental.pallas import tpu as pltpu
from jax.sharding import PartitionSpec as P

DAMPING = 0.5
EPSILON = 1e-05
F32 = jnp.float32
BF = jnp.bfloat16
MESH = pl.DeviceIdType.MESH
ANY = pl.BlockSpec(memory_space=pl.ANY)
VM = pl.BlockSpec(memory_space=pltpu.VMEM)

NX, NY, NZ = 4, 4, 2
NP = 8
NS = 16
ROWS = 640
COLS = 256
WIDE = 2 * ROWS
CH = 4
B = 128


def place():
    s, p = lax.axis_index("samp"), lax.axis_index("par")
    return s, p


class Copies:
    def __init__(self):
        self.sent = []

    def send(self, src, dst, send_sem, recv_sem, s, p, cond=None):
        copy = pltpu.make_async_remote_copy(
            src_ref=src,
            dst_ref=dst,
            send_sem=send_sem,
            recv_sem=recv_sem,
            device_id={"samp": s, "par": p},
            device_id_type=MESH,
        )
        if cond is None:
            copy.start()
        else:
            pl.when(cond)(copy.start)
        self.sent.append((cond, copy))

    def drain(self):
        for cond, copy in self.sent:
            if cond is None:
                copy.wait_send()
            else:
                pl.when(cond)(copy.wait_send)


def arrived(ref, sem):
    pltpu.make_async_copy(ref, ref, sem).wait()


def greet(s, p):
    barrier = pltpu.get_barrier_semaphore()
    for i in range(1, NS):
        pl.semaphore_signal(
            barrier, inc=1, device_id={"samp": lax.rem(s + i, NS), "par": p}, device_id_type=MESH
        )
    for i in range(1, NP):
        pl.semaphore_signal(
            barrier, inc=1, device_id={"samp": s, "par": lax.rem(p + i, NP)}, device_id_type=MESH
        )
    pl.semaphore_wait(barrier, NS + NP - 2)


def first_kernel(
    act, sig, sig_rows, a0, sig_all, stat_all,
    mom, moms, sigs, stat, stats,
    own_sem, one_send, one_recv, two_send, two_recv, core_send, core_recv,
    mom_send, mom_recv, sig_send, sig_recv, stat_send, stat_recv,
):
    s, p = place()
    c, k = lax.rem(s, 2), s // 2
    x, zh = lax.rem(k, NX), k // NX
    y, zl = p // NZ, lax.rem(p, NZ)
    other = s + 1 - 2 * c
    step = ROWS // CH

    def samp_of(zz, xx):
        return 2 * (zz * NX + xx) + c

    def par_of(yy, ll):
        return yy * NZ + ll

    up, down = lax.rem(y + 1, NY), lax.rem(y + NY - 1, NY)
    far, lo = lax.rem(y + 2, NY), 1 - zl
    ahead = jnp.where(c == 0, up, down)
    behind = jnp.where(c == 0, down, up)
    net = Copies()

    def part(q, t):
        return a0.at[c, q, pl.ds(t * step, step), :]

    own_copy = pltpu.make_async_copy(act, a0.at[c, p], own_sem)

    @pl.when(k == 0)
    def _():
        own_copy.start()

    greet(s, p)

    @pl.when(k == 0)
    def _():
        own_copy.wait()

    def stage_own(t):
        @pl.when(k > 0)
        def _():
            arrived(part(p, t), one_recv.at[t])

        net.send(part(p, t), part(p, t), one_send.at[0, t], one_recv.at[t], samp_of(zh, 1), p, x == 0)
        net.send(part(p, t), part(p, t), one_send.at[1, t], one_recv.at[t], samp_of(zh, 3), p, x == 0)
        net.send(part(p, t), part(p, t), one_send.at[2, t], one_recv.at[t], samp_of(1, 0), p, k == 0)
        relay = jnp.logical_or(
            jnp.logical_and(x == 1, c == 0), jnp.logical_and(x == 3, c == 1)
        )
        net.send(part(p, t), part(p, t), one_send.at[3, t], one_recv.at[t], samp_of(zh, 2), p, relay)
        net.send(part(p, t), part(p, t), two_send.at[0, t], two_recv.at[0, t], s, par_of(y, lo))
        net.send(part(p, t), part(p, t), two_send.at[1, t], two_recv.at[1, t], s, par_of(up, zl))
        net.send(part(p, t), part(p, t), two_send.at[2, t], two_recv.at[2, t], s, par_of(down, zl))
        net.send(part(p, t), part(p, t), core_send.at[0, t], core_recv.at[0, t], other, p)

    def stage_near(t):
        q = par_of(y, lo)
        arrived(part(q, t), two_recv.at[0, t])
        net.send(part(q, t), part(q, t), two_send.at[3, t], two_recv.at[3, t], s, par_of(up, zl))
        net.send(part(q, t), part(q, t), two_send.at[4, t], two_recv.at[4, t], s, par_of(down, zl))
        net.send(part(q, t), part(q, t), core_send.at[1, t], core_recv.at[1, t], other, p)
        qu, qd = par_of(down, zl), par_of(up, zl)
        arrived(part(qu, t), two_recv.at[1, t])
        arrived(part(qd, t), two_recv.at[2, t])
        qb = par_of(behind, zl)
        net.send(part(qb, t), part(qb, t), two_send.at[5, t], two_recv.at[5, t], s, par_of(ahead, zl))
        net.send(part(qu, t), part(qu, t), core_send.at[2, t], core_recv.at[2, t], other, p)
        net.send(part(qd, t), part(qd, t), core_send.at[3, t], core_recv.at[3, t], other, p)

    def stage_far(t):
        q = par_of(far, zl)
        arrived(part(q, t), two_recv.at[5, t])
        net.send(part(q, t), part(q, t), two_send.at[6, t], two_recv.at[6, t], s, par_of(y, lo))
        net.send(part(q, t), part(q, t), core_send.at[4, t], core_recv.at[4, t], other, p)
        qu, qd = par_of(down, lo), par_of(up, lo)
        arrived(part(qu, t), two_recv.at[3, t])
        arrived(part(qd, t), two_recv.at[4, t])
        net.send(part(qu, t), part(qu, t), core_send.at[5, t], core_recv.at[5, t], other, p)
        net.send(part(qd, t), part(qd, t), core_send.at[6, t], core_recv.at[6, t], other, p)

    def stage_last(t):
        q = par_of(far, lo)
        arrived(part(q, t), two_recv.at[6, t])
        net.send(part(q, t), part(q, t), core_send.at[7, t], core_recv.at[7, t], other, p)

    for i in range(1, NS):
        net.send(sig_rows, sigs.at[s], sig_send.at[i], sig_recv.at[s], lax.rem(s + i, NS), p)

    @pl.when(k == 0)
    def _():
        pass

    def add(i, sums):
        rows = pl.ds(pl.multiple_of(i * 80, 80), 80)
        a = act[rows, :].astype(F32)
        g = sig[rows, :]
        new = []
        for o in range(2):
            v = g[:, o : o + 1] * a
            new.append(sums[2 * o] + jnp.sum(v.reshape(10, 8, COLS), axis=0))
            new.append(sums[2 * o + 1] + jnp.sum((v * v).reshape(10, 8, COLS), axis=0))
        return tuple(new)

    stage_own(0)
    zero = jnp.zeros((8, COLS), F32)
    sums = lax.fori_loop(0, ROWS // 80, add, (zero,) * 4)
    mom[...] = jnp.concatenate(
        [jnp.sum(v, axis=0, keepdims=True) for v in sums] + [jnp.zeros((4, COLS), F32)], axis=0
    )
    for i in range(1, NS):
        net.send(mom, moms.at[s], mom_send.at[i], mom_recv.at[s], lax.rem(s + i, NS), p)
    moms[s] = mom[...]
    sigs[s] = sig_rows[...]

    for t in range(1, CH + 3):
        if t < CH:
            stage_own(t)
        if t == 1:
            for i in range(1, NS):
                j = lax.rem(s + i, NS)
                arrived(moms.at[j], mom_recv.at[j])
            total = moms[0]
            for j in range(1, NS):
                total = total + moms[j]
            count, width = float(NS * ROWS), float(2 * COLS * NP)
            rows = []
            for o in range(2):
                average = total[2 * o : 2 * o + 1] / count
                second = total[2 * o + 1 : 2 * o + 2] / count
                scale = 1.0 / jnp.sqrt(width * (second - average * average + EPSILON))
                rows += [average, scale]
            stat[...] = jnp.concatenate(rows + [jnp.zeros((4, COLS), F32)], axis=0)
            for i in range(1, NP):
                net.send(stat, stats.at[p], stat_send.at[i], stat_recv.at[p], s, lax.rem(p + i, NP))
            stats[p] = stat[...]
        if 0 <= t - 1 < CH:
            stage_near(t - 1)
        if 0 <= t - 2 < CH:
            stage_far(t - 2)
        if 0 <= t - 3 < CH:
            stage_last(t - 3)

    for i in range(1, NS):
        j = lax.rem(s + i, NS)
        arrived(sigs.at[j], sig_recv.at[j])
    for i in range(1, NP):
        j = lax.rem(p + i, NP)
        arrived(stats.at[j], stat_recv.at[j])
    sig_all[...] = sigs[...]
    stat_all[...] = stats[...]
    order = [
        (y, zl), (y, lo), (down, zl), (up, zl), (far, zl), (down, lo), (up, lo), (far, lo),
    ]
    for t in range(CH):
        for n, (yy, ll) in enumerate(order):
            arrived(a0.at[1 - c, par_of(yy, ll), pl.ds(t * step, step), :], core_recv.at[n, t])
    net.drain()


def gather_first(act, sig, sig_rows):
    dma = pltpu.SemaphoreType.DMA
    return pl.pallas_call(
        first_kernel,
        name="gather_first",
        out_shape=(
            jax.ShapeDtypeStruct((2, NP, ROWS, COLS), BF),
            jax.ShapeDtypeStruct((NS, 8, ROWS), F32),
            jax.ShapeDtypeStruct((NP, 8, COLS), F32),
        ),
        in_specs=[VM, VM, VM],
        out_specs=(ANY, VM, VM),
        scratch_shapes=[
            pltpu.VMEM((8, COLS), F32),
            pltpu.VMEM((NS, 8, COLS), F32),
            pltpu.VMEM((NS, 8, ROWS), F32),
            pltpu.VMEM((8, COLS), F32),
            pltpu.VMEM((NP, 8, COLS), F32),
            dma, dma((4, CH)), dma((CH,)), dma((7, CH)), dma((7, CH)), dma((8, CH)), dma((8, CH)),
            dma((NS,)), dma((NS,)), dma((NS,)), dma((NS,)), dma((NP,)), dma((NP,)),
        ],
        compiler_params=pltpu.CompilerParams(collective_id=0, has_side_effects=True),
    )(act, sig, sig_rows)


def rest_kernel(
    act, ar, ac, kbuf,
    own_sem, row_send, row_recv, col_send, col_recv, two_send, two_recv, core_send, core_recv,
):
    s, p = place()
    c, k = lax.rem(s, 2), s // 2
    other = s + 1 - 2 * c
    net = Copies()
    own = [
        pltpu.make_async_copy(act, ar.at[p], own_sem.at[0]),
        pltpu.make_async_copy(act, kbuf.at[k], own_sem.at[1]),
    ]
    for copy in own:
        copy.start()
    greet(s, p)
    for i in range(1, NP):
        to = lax.rem(k + i, NP)
        net.send(act, kbuf.at[k], col_send.at[i], col_recv.at[k], 2 * to + c, p)
    for i in range(1, NP):
        net.send(act, ar.at[p], row_send.at[i], row_recv.at[p], s, lax.rem(p + i, NP))
    for copy in own:
        copy.wait()
    for i in range(1, NP):
        j = lax.rem(k + i, NP)
        arrived(kbuf.at[j], col_recv.at[j])
    mine = pltpu.make_async_copy(kbuf.at[p], ac.at[c, p], own_sem.at[2])
    mine.start()
    for i in range(1, NP):
        to = lax.rem(p + i, NP)
        net.send(kbuf.at[to], ac.at[c, p], two_send.at[i], two_recv.at[p], s, to)
    mine.wait()
    for i in range(NP):
        j = lax.rem(p + i, NP)
        if i:
            arrived(ac.at[c, j], two_recv.at[j])
        net.send(ac.at[c, j], ac.at[c, j], core_send.at[i], core_recv.at[j], other, p)
    for i in range(1, NP):
        j = lax.rem(p + i, NP)
        arrived(ar.at[j], row_recv.at[j])
    for j in range(NP):
        arrived(ac.at[1 - c, j], core_recv.at[j])
    net.drain()


def gather_rest(act):
    dma = pltpu.SemaphoreType.DMA
    return pl.pallas_call(
        rest_kernel,
        name="gather_rest",
        out_shape=(
            jax.ShapeDtypeStruct((NP, ROWS, COLS), BF),
            jax.ShapeDtypeStruct((2, NP, ROWS, COLS), BF),
        ),
        in_specs=[VM],
        out_specs=(ANY, ANY),
        scratch_shapes=[
            pltpu.VMEM((NP, ROWS, COLS), BF),
            dma((3,)), dma((NP,)), dma((NP,)), dma((NP,)), dma((NP,)), dma((NP,)), dma((NP,)),
            dma((NP,)), dma((NP,)),
        ],
        compiler_params=pltpu.CompilerParams(collective_id=1, has_side_effects=True),
    )(act)


def split(v):
    hi = v.astype(BF)
    return hi, (v - hi.astype(F32)).astype(BF)


def dot3(a, b, ca, cb):
    dims = (((ca,), (cb,)), ((), ()))

    def one(u, v):
        return lax.dot_general(u, v, dims, preferred_element_type=F32)

    return one(a[0], b[1]) + one(a[1], b[0]) + one(a[0], b[0])


def dot1(a, b):
    return lax.dot_general(a, b, (((1,), (1,)), ((), ())), preferred_element_type=F32)


def row(v, i):
    return jnp.broadcast_to(v[i : i + 1, :], (8, B))


def lane(v, i):
    return jnp.broadcast_to(v[:, i : i + 1], (8, B))


def leaf(tiles, eye, sub):
    out = []
    for m in range(len(tiles)):
        top, unit = tiles[m], eye[m]
        cols = [[lane(tiles[i], 8 * m + b) for b in range(8)] for i in range(m, len(tiles))]
        scale, factors = None, []
        for k in range(8):
            r = lax.rsqrt(row(cols[0][k], k))
            inv = r * r
            scale = r if scale is None else jnp.where(sub == k, r, scale)
            pivots = [row(cols[0][k], b) for b in range(k + 1, 8)]
            f = [v[k] * inv for v in cols]
            for v, g in zip(cols, f):
                for b in range(k + 1, 8):
                    v[b] = v[b] - g * pivots[b - k - 1]
            if k < 7:
                below = jnp.where(sub > k, f[0], 0.0)
                top = top - below * row(top, k)
                unit = unit - below * row(unit, k)
            factors.append(f[1:])
        for n, i in enumerate(range(m + 1, len(tiles))):
            da = functools.reduce(jnp.add, [factors[k][n] * row(top, k) for k in range(8)])
            du = functools.reduce(jnp.add, [factors[k][n] * row(unit, k) for k in range(8)])
            tiles[i] = tiles[i] - da
            eye[i] = eye[i] - du
        out.append(unit * scale)
    return out


def factor_inverse(z, inv_block):
    n = z.shape[0]
    nb = n // B
    sub = lax.broadcasted_iota(jnp.int32, (8, B), 0)
    ln = lax.broadcasted_iota(jnp.int32, (8, B), 1)

    def body(j, carry):
        j0 = pl.multiple_of(j * B, B)
        here = pl.ds(j0, B)
        tiles = [z[pl.ds(pl.multiple_of(j0 + 8 * i, 8), 8), here] for i in range(B // 8)]
        eye = [jnp.where(ln == sub + 8 * i, 1.0, 0.0).astype(F32) for i in range(B // 8)]
        for i, v in enumerate(leaf(tiles, eye, sub)):
            inv_block[8 * i : 8 * i + 8, :] = v
        w = inv_block[...]
        z[here, :] = dot3(split(w), split(z[here, :]), 1, 0)
        z[here, here] = w
        for jj in range(nb - 1):

            @pl.when(j == jj)
            def _():
                y = split(z[jj * B : jj * B + B, :])
                low = (jj + 1) * B
                z[low:, jj * B : low] = jnp.zeros((n - low, B), F32)
                for t in range(jj + 1, nb):
                    rows = slice(t * B, t * B + B)
                    z[rows, :] = z[rows, :] - dot3((y[0][:, rows], y[1][:, rows]), y, 0, 0)

        return carry

    lax.fori_loop(0, nb, body, 0)


def fill(dst, base, act, sig_cols, stat):
    a = act.astype(F32)
    for o in range(2):
        v = sig_cols[:, o : o + 1] * a
        v = (v - stat[2 * o : 2 * o + 1]) * stat[2 * o + 1 : 2 * o + 2]
        dst[base : base + ROWS, o * COLS : (o + 1) * COLS] = v.astype(BF)


def cols_of(rows):
    return jnp.transpose(rows)


def factor_kernel(a0, sig_all, stat_all, w_out, z, jac, sig_cols, inv_block, sem):
    q = pl.program_id(0)

    @pl.when(q == 0)
    def _():
        for h in range(2):
            sig_cols[h] = cols_of(sig_all[h])
        z[...] = jnp.zeros_like(z)

    for h in range(2):
        fill(jac, h * ROWS, a0[h, 0], sig_cols[h], stat_all[0])
    for r in range(WIDE // COLS):
        rows = slice(r * COLS, (r + 1) * COLS)
        z[rows, r * COLS :] += dot1(jac[rows, :], jac[r * COLS :, :])

    @pl.when(q == NP - 1)
    def _():
        for r in range(WIDE // B):
            rows = slice(r * B, (r + 1) * B)
            i = lax.broadcasted_iota(jnp.int32, (B, B), 0)
            j = lax.broadcasted_iota(jnp.int32, (B, B), 1)
            z[rows, rows] += jnp.where(i == j, DAMPING, 0.0).astype(F32)
        factor_inverse(z, inv_block)
        copy = pltpu.make_async_copy(z, w_out, sem)
        copy.start()
        copy.wait()


def factor(a0, sig_all, stat_all):
    return pl.pallas_call(
        factor_kernel,
        name="factor",
        grid=(NP,),
        out_shape=jax.ShapeDtypeStruct((WIDE, WIDE), F32),
        in_specs=[
            pl.BlockSpec((2, 1, ROWS, COLS), lambda q: (0, q, 0, 0)),
            pl.BlockSpec((2, 8, ROWS), lambda q: (0, 0, 0)),
            pl.BlockSpec((1, 8, COLS), lambda q: (q, 0, 0)),
        ],
        out_specs=ANY,
        scratch_shapes=[
            pltpu.VMEM((WIDE, WIDE), F32),
            pltpu.VMEM((WIDE, 2 * COLS), BF),
            pltpu.VMEM((2, ROWS, 8), F32),
            pltpu.VMEM((B, B), F32),
            pltpu.SemaphoreType.DMA,
        ],
        compiler_params=pltpu.CompilerParams(vmem_limit_bytes=56 * 2**20),
    )(a0, sig_all, stat_all)


def final_kernel(
    ar, ac, a0, sig_all, stat_all, w_all, gram, panel,
    lead, jr, jc, j0, sig_r, sig_c, sig_0, w, sem,
):
    q = pl.program_id(0)
    s, p = place()
    width = WIDE // NP

    fetch = pltpu.make_async_copy(
        w_all.at[pl.ds(pl.multiple_of(p * width, 8), width), :], w, sem
    )

    @pl.when(q == 0)
    def _():
        fetch.start()
        sig_r[...] = cols_of(sig_all[s])
        for h in range(2):
            sig_c[h] = cols_of(sig_all[2 * p + h])
            sig_0[h] = cols_of(sig_all[h])
        gram[...] = jnp.zeros_like(gram)
        lead[...] = jnp.zeros_like(lead)

    stat = stat_all[0]
    fill(jr, 0, ar[0], sig_r, stat)
    for h in range(2):
        fill(jc, h * ROWS, ac[h, 0], sig_c[h], stat)
        fill(j0, h * ROWS, a0[h, 0], sig_0[h], stat)
    gram[...] += dot1(jr[...], jc[...])
    lead[...] += dot1(jr[...], j0[...])

    @pl.when(q == NP - 1)
    def _():
        i = lax.broadcasted_iota(jnp.int32, (ROWS, WIDE), 0) + s * ROWS
        j = lax.broadcasted_iota(jnp.int32, (ROWS, WIDE), 1)
        gram[...] += jnp.where(i == j + p * WIDE, DAMPING, 0.0).astype(F32)
        g = lead[...] + jnp.where(i == j, DAMPING, 0.0).astype(F32)
        fetch.wait()
        wi = lax.broadcasted_iota(jnp.int32, (width, WIDE), 0) + p * width
        wj = lax.broadcasted_iota(jnp.int32, (width, WIDE), 1)
        low = jnp.where(wj <= wi, w[...], 0.0)
        out = dot3(split(g), split(low), 1, 1)
        skip = jnp.logical_and(s == 0, p >= NP // 2)
        panel[...] = jnp.where(skip, 0.0, out)


def finish(ar, ac, a0, sig_all, stat_all, w_all):
    whole = lambda *shape: pl.BlockSpec(shape, lambda q: (0,) * len(shape))
    return pl.pallas_call(
        final_kernel,
        name="finish",
        grid=(NP,),
        out_shape=(
            jax.ShapeDtypeStruct((ROWS, WIDE), F32),
            jax.ShapeDtypeStruct((ROWS, WIDE // NP), F32),
        ),
        in_specs=[
            pl.BlockSpec((1, ROWS, COLS), lambda q: (q, 0, 0)),
            pl.BlockSpec((2, 1, ROWS, COLS), lambda q: (0, q, 0, 0)),
            pl.BlockSpec((2, 1, ROWS, COLS), lambda q: (0, q, 0, 0)),
            whole(NS, 8, ROWS),
            pl.BlockSpec((1, 8, COLS), lambda q: (q, 0, 0)),
            ANY,
        ],
        out_specs=(whole(ROWS, WIDE), whole(ROWS, WIDE // NP)),
        scratch_shapes=[
            pltpu.VMEM((ROWS, WIDE), F32),
            pltpu.VMEM((ROWS, 2 * COLS), BF),
            pltpu.VMEM((WIDE, 2 * COLS), BF),
            pltpu.VMEM((WIDE, 2 * COLS), BF),
            pltpu.VMEM((ROWS, 8), F32),
            pltpu.VMEM((2, ROWS, 8), F32),
            pltpu.VMEM((2, ROWS, 8), F32),
            pltpu.VMEM((WIDE // NP, WIDE), F32),
            pltpu.SemaphoreType.DMA,
        ],
        compiler_params=pltpu.CompilerParams(vmem_limit_bytes=56 * 2**20),
    )(ar, ac, a0, sig_all, stat_all, w_all)


def per_device(activations, signal):
    sig = signal.astype(F32)
    sig_rows = jnp.pad(sig.T, ((0, 6), (0, 0)))
    a0, sig_all, stat_all = gather_first(activations, sig, sig_rows)
    ar, ac = gather_rest(activations)
    w = factor(a0, sig_all, stat_all)
    return finish(ar, ac, a0, sig_all, stat_all, w)


def solution(mesh):
    return jax.shard_map(
        per_device,
        mesh=mesh,
        in_specs=(P("samp", "par"), P("samp", None)),
        out_specs=(P("samp", "par"), P("samp", "par")),
        check_vma=False,
    )
```

```python
import functools

import jax
import jax.numpy as jnp
from jax import lax
from jax.experimental import pallas as pl
from jax.experimental.pallas import tpu as pltpu
from jax.sharding import PartitionSpec as P

DAMPING = 0.5
EPSILON = 1e-05
F32 = jnp.float32
BF = jnp.bfloat16
MESH = pl.DeviceIdType.MESH
ANY = pl.BlockSpec(memory_space=pl.ANY)
VM = pl.BlockSpec(memory_space=pltpu.VMEM)

NX, NY, NZ = 4, 4, 2
NP = 8
NS = 16
ROWS = 640
COLS = 256
WIDE = 2 * ROWS
CH = 4
B = 128


def place():
    s, p = lax.axis_index("samp"), lax.axis_index("par")
    return s, p


class Copies:
    def __init__(self):
        self.sent = []

    def send(self, src, dst, send_sem, recv_sem, s, p, cond=None):
        copy = pltpu.make_async_remote_copy(
            src_ref=src,
            dst_ref=dst,
            send_sem=send_sem,
            recv_sem=recv_sem,
            device_id={"samp": s, "par": p},
            device_id_type=MESH,
        )
        if cond is None:
            copy.start()
        else:
            pl.when(cond)(copy.start)
        self.sent.append((cond, copy))

    def drain(self):
        for cond, copy in self.sent:
            if cond is None:
                copy.wait_send()
            else:
                pl.when(cond)(copy.wait_send)


def arrived(ref, sem):
    pltpu.make_async_copy(ref, ref, sem).wait()


def greet(s, p):
    barrier = pltpu.get_barrier_semaphore()
    for i in range(1, NS):
        pl.semaphore_signal(
            barrier, inc=1, device_id={"samp": lax.rem(s + i, NS), "par": p}, device_id_type=MESH
        )
    for i in range(1, NP):
        pl.semaphore_signal(
            barrier, inc=1, device_id={"samp": s, "par": lax.rem(p + i, NP)}, device_id_type=MESH
        )
    pl.semaphore_wait(barrier, NS + NP - 2)


def first_kernel(
    act, sig, sig_rows, a0, sig_all, stat_all,
    mom, moms, sigs, stat, stats,
    own_sem, one_send, one_recv, two_send, two_recv, core_send, core_recv,
    mom_send, mom_recv, sig_send, sig_recv, stat_send, stat_recv,
):
    s, p = place()
    c, k = lax.rem(s, 2), s // 2
    x, zh = lax.rem(k, NX), k // NX
    y, zl = p // NZ, lax.rem(p, NZ)
    other = s + 1 - 2 * c
    step = ROWS // CH

    def samp_of(zz, xx):
        return 2 * (zz * NX + xx) + c

    def par_of(yy, ll):
        return yy * NZ + ll

    up, down = lax.rem(y + 1, NY), lax.rem(y + NY - 1, NY)
    far, lo = lax.rem(y + 2, NY), 1 - zl
    ahead = jnp.where(c == 0, up, down)
    behind = jnp.where(c == 0, down, up)
    net = Copies()

    def part(q, t):
        return a0.at[c, q, pl.ds(t * step, step), :]

    own_copy = pltpu.make_async_copy(act, a0.at[c, p], own_sem)

    @pl.when(k == 0)
    def _():
        own_copy.start()

    greet(s, p)

    @pl.when(k == 0)
    def _():
        own_copy.wait()

    def stage_own(t):
        @pl.when(k > 0)
        def _():
            arrived(part(p, t), one_recv.at[t])

        net.send(part(p, t), part(p, t), one_send.at[0, t], one_recv.at[t], samp_of(zh, 1), p, x == 0)
        net.send(part(p, t), part(p, t), one_send.at[1, t], one_recv.at[t], samp_of(zh, 3), p, x == 0)
        net.send(part(p, t), part(p, t), one_send.at[2, t], one_recv.at[t], samp_of(1, 0), p, k == 0)
        relay = jnp.logical_or(
            jnp.logical_and(x == 1, c == 0), jnp.logical_and(x == 3, c == 1)
        )
        net.send(part(p, t), part(p, t), one_send.at[3, t], one_recv.at[t], samp_of(zh, 2), p, relay)
        net.send(part(p, t), part(p, t), two_send.at[0, t], two_recv.at[0, t], s, par_of(y, lo))
        net.send(part(p, t), part(p, t), two_send.at[1, t], two_recv.at[1, t], s, par_of(up, zl))
        net.send(part(p, t), part(p, t), two_send.at[2, t], two_recv.at[2, t], s, par_of(down, zl))
        net.send(part(p, t), part(p, t), core_send.at[0, t], core_recv.at[0, t], other, p)

    def stage_near(t):
        q = par_of(y, lo)
        arrived(part(q, t), two_recv.at[0, t])
        net.send(part(q, t), part(q, t), two_send.at[3, t], two_recv.at[3, t], s, par_of(up, zl))
        net.send(part(q, t), part(q, t), two_send.at[4, t], two_recv.at[4, t], s, par_of(down, zl))
        net.send(part(q, t), part(q, t), core_send.at[1, t], core_recv.at[1, t], other, p)
        qu, qd = par_of(down, zl), par_of(up, zl)
        arrived(part(qu, t), two_recv.at[1, t])
        arrived(part(qd, t), two_recv.at[2, t])
        qb = par_of(behind, zl)
        net.send(part(qb, t), part(qb, t), two_send.at[5, t], two_recv.at[5, t], s, par_of(ahead, zl))
        net.send(part(qu, t), part(qu, t), core_send.at[2, t], core_recv.at[2, t], other, p)
        net.send(part(qd, t), part(qd, t), core_send.at[3, t], core_recv.at[3, t], other, p)

    def stage_far(t):
        q = par_of(far, zl)
        arrived(part(q, t), two_recv.at[5, t])
        net.send(part(q, t), part(q, t), two_send.at[6, t], two_recv.at[6, t], s, par_of(y, lo))
        net.send(part(q, t), part(q, t), core_send.at[4, t], core_recv.at[4, t], other, p)
        qu, qd = par_of(down, lo), par_of(up, lo)
        arrived(part(qu, t), two_recv.at[3, t])
        arrived(part(qd, t), two_recv.at[4, t])
        net.send(part(qu, t), part(qu, t), core_send.at[5, t], core_recv.at[5, t], other, p)
        net.send(part(qd, t), part(qd, t), core_send.at[6, t], core_recv.at[6, t], other, p)

    def stage_last(t):
        q = par_of(far, lo)
        arrived(part(q, t), two_recv.at[6, t])
        net.send(part(q, t), part(q, t), core_send.at[7, t], core_recv.at[7, t], other, p)

    for i in range(1, NS):
        net.send(sig_rows, sigs.at[s], sig_send.at[i], sig_recv.at[s], lax.rem(s + i, NS), p)

    @pl.when(k == 0)
    def _():
        pass

    def add(i, sums):
        rows = pl.ds(pl.multiple_of(i * 80, 80), 80)
        a = act[rows, :].astype(F32)
        g = sig[rows, :]
        new = []
        for o in range(2):
            v = g[:, o : o + 1] * a
            new.append(sums[2 * o] + jnp.sum(v.reshape(10, 8, COLS), axis=0))
            new.append(sums[2 * o + 1] + jnp.sum((v * v).reshape(10, 8, COLS), axis=0))
        return tuple(new)

    stage_own(0)
    zero = jnp.zeros((8, COLS), F32)
    sums = lax.fori_loop(0, ROWS // 80, add, (zero,) * 4)
    mom[...] = jnp.concatenate(
        [jnp.sum(v, axis=0, keepdims=True) for v in sums] + [jnp.zeros((4, COLS), F32)], axis=0
    )
    for i in range(1, NS):
        net.send(mom, moms.at[s], mom_send.at[i], mom_recv.at[s], lax.rem(s + i, NS), p)
    moms[s] = mom[...]
    sigs[s] = sig_rows[...]

    for t in range(1, CH + 3):
        if t < CH:
            stage_own(t)
        if t == 1:
            for i in range(1, NS):
                j = lax.rem(s + i, NS)
                arrived(moms.at[j], mom_recv.at[j])
            total = moms[0]
            for j in range(1, NS):
                total = total + moms[j]
            count, width = float(NS * ROWS), float(2 * COLS * NP)
            rows = []
            for o in range(2):
                average = total[2 * o : 2 * o + 1] / count
                second = total[2 * o + 1 : 2 * o + 2] / count
                scale = 1.0 / jnp.sqrt(width * (second - average * average + EPSILON))
                rows += [average, scale]
            stat[...] = jnp.concatenate(rows + [jnp.zeros((4, COLS), F32)], axis=0)
            for i in range(1, NP):
                net.send(stat, stats.at[p], stat_send.at[i], stat_recv.at[p], s, lax.rem(p + i, NP))
            stats[p] = stat[...]
        if 0 <= t - 1 < CH:
            stage_near(t - 1)
        if 0 <= t - 2 < CH:
            stage_far(t - 2)
        if 0 <= t - 3 < CH:
            stage_last(t - 3)

    for i in range(1, NS):
        j = lax.rem(s + i, NS)
        arrived(sigs.at[j], sig_recv.at[j])
    for i in range(1, NP):
        j = lax.rem(p + i, NP)
        arrived(stats.at[j], stat_recv.at[j])
    sig_all[...] = sigs[...]
    stat_all[...] = stats[...]
    order = [
        (y, zl), (y, lo), (down, zl), (up, zl), (far, zl), (down, lo), (up, lo), (far, lo),
    ]
    for t in range(CH):
        for n, (yy, ll) in enumerate(order):
            arrived(a0.at[1 - c, par_of(yy, ll), pl.ds(t * step, step), :], core_recv.at[n, t])
    net.drain()


def gather_first(act, sig, sig_rows):
    dma = pltpu.SemaphoreType.DMA
    return pl.pallas_call(
        first_kernel,
        name="gather_first",
        out_shape=(
            jax.ShapeDtypeStruct((2, NP, ROWS, COLS), BF),
            jax.ShapeDtypeStruct((NS, 8, ROWS), F32),
            jax.ShapeDtypeStruct((NP, 8, COLS), F32),
        ),
        in_specs=[VM, VM, VM],
        out_specs=(ANY, VM, VM),
        scratch_shapes=[
            pltpu.VMEM((8, COLS), F32),
            pltpu.VMEM((NS, 8, COLS), F32),
            pltpu.VMEM((NS, 8, ROWS), F32),
            pltpu.VMEM((8, COLS), F32),
            pltpu.VMEM((NP, 8, COLS), F32),
            dma, dma((4, CH)), dma((CH,)), dma((7, CH)), dma((7, CH)), dma((8, CH)), dma((8, CH)),
            dma((NS,)), dma((NS,)), dma((NS,)), dma((NS,)), dma((NP,)), dma((NP,)),
        ],
        compiler_params=pltpu.CompilerParams(collective_id=0, has_side_effects=True),
    )(act, sig, sig_rows)


class Rest:
    def __init__(self, act, ar, ac, kbuf, sems):
        (own_sem, row_send, row_recv, col_send, col_recv, two_send, two_recv, core_send, core_recv) = sems
        s, p = place()
        c, k = lax.rem(s, 2), s // 2
        other = s + 1 - 2 * c
        self.own = [
            pltpu.make_async_copy(act, ar.at[p], own_sem.at[0]),
            pltpu.make_async_copy(act, kbuf.at[k], own_sem.at[1]),
            pltpu.make_async_copy(kbuf.at[p], ac.at[c, p], own_sem.at[2]),
        ]
        self.col, self.row, self.two, self.core = [], [], [], []
        self.col_in, self.row_in, self.two_in, self.core_in = [], [], [], []
        for i in range(1, NP):
            to, on = lax.rem(k + i, NP), lax.rem(p + i, NP)
            self.col.append(far_copy(act, kbuf.at[k], col_send.at[i], col_recv.at[k], 2 * to + c, p))
            self.row.append(far_copy(act, ar.at[p], row_send.at[i], row_recv.at[p], s, on))
            self.two.append(far_copy(kbuf.at[on], ac.at[c, p], two_send.at[i], two_recv.at[p], s, on))
            self.col_in.append((kbuf.at[to], col_recv.at[to]))
            self.row_in.append((ar.at[on], row_recv.at[on]))
            self.two_in.append((ac.at[c, on], two_recv.at[on]))
        for i in range(NP):
            on = lax.rem(p + i, NP)
            self.core.append(far_copy(ac.at[c, on], ac.at[c, on], core_send.at[i], core_recv.at[on], other, p))
            self.core_in.append((ac.at[1 - c, i], core_recv.at[i]))

    def begin(self):
        s, p = place()
        self.own[0].start()
        self.own[1].start()
        greet(s, p)
        for copy in self.col + self.row:
            copy.start()

    def second(self):
        self.own[0].wait()
        self.own[1].wait()
        for ref, sem in self.col_in:
            arrived(ref, sem)
        for copy in self.two + [self.own[2]]:
            copy.start()

    def third(self):
        self.own[2].wait()
        self.core[0].start()
        for (ref, sem), copy in zip(self.two_in, self.core[1:]):
            arrived(ref, sem)
            copy.start()

    def end(self):
        for ref, sem in self.row_in + self.core_in:
            arrived(ref, sem)
        for copy in self.col + self.row + self.two + self.core:
            copy.wait_send()


def far_copy(src, dst, send_sem, recv_sem, s, p):
    return pltpu.make_async_remote_copy(
        src_ref=src,
        dst_ref=dst,
        send_sem=send_sem,
        recv_sem=recv_sem,
        device_id={"samp": s, "par": p},
        device_id_type=MESH,
    )


def split(v):
    hi = v.astype(BF)
    return hi, (v - hi.astype(F32)).astype(BF)


def dot3(a, b, ca, cb):
    dims = (((ca,), (cb,)), ((), ()))

    def one(u, v):
        return lax.dot_general(u, v, dims, preferred_element_type=F32)

    return one(a[0], b[1]) + one(a[1], b[0]) + one(a[0], b[0])


def dot1(a, b):
    return lax.dot_general(a, b, (((1,), (1,)), ((), ())), preferred_element_type=F32)


def row(v, i):
    return jnp.broadcast_to(v[i : i + 1, :], (8, B))


def lane(v, i):
    return jnp.broadcast_to(v[:, i : i + 1], (8, B))


def leaf(tiles, eye, sub):
    out = []
    for m in range(len(tiles)):
        top, unit = tiles[m], eye[m]
        cols = [[lane(tiles[i], 8 * m + b) for b in range(8)] for i in range(m, len(tiles))]
        scale, factors = None, []
        for k in range(8):
            r = lax.rsqrt(row(cols[0][k], k))
            inv = r * r
            scale = r if scale is None else jnp.where(sub == k, r, scale)
            pivots = [row(cols[0][k], b) for b in range(k + 1, 8)]
            f = [v[k] * inv for v in cols]
            for v, g in zip(cols, f):
                for b in range(k + 1, 8):
                    v[b] = v[b] - g * pivots[b - k - 1]
            if k < 7:
                below = jnp.where(sub > k, f[0], 0.0)
                top = top - below * row(top, k)
                unit = unit - below * row(unit, k)
            factors.append(f[1:])
        for n, i in enumerate(range(m + 1, len(tiles))):
            da = functools.reduce(jnp.add, [factors[k][n] * row(top, k) for k in range(8)])
            du = functools.reduce(jnp.add, [factors[k][n] * row(unit, k) for k in range(8)])
            tiles[i] = tiles[i] - da
            eye[i] = eye[i] - du
        out.append(unit * scale)
    return out


def factor_inverse(z, inv_block, between):
    n = z.shape[0]
    nb = n // B
    sub = lax.broadcasted_iota(jnp.int32, (8, B), 0)
    ln = lax.broadcasted_iota(jnp.int32, (8, B), 1)

    def body(j, carry):
        between(j)
        j0 = pl.multiple_of(j * B, B)
        here = pl.ds(j0, B)
        tiles = [z[pl.ds(pl.multiple_of(j0 + 8 * i, 8), 8), here] for i in range(B // 8)]
        eye = [jnp.where(ln == sub + 8 * i, 1.0, 0.0).astype(F32) for i in range(B // 8)]
        for i, v in enumerate(leaf(tiles, eye, sub)):
            inv_block[8 * i : 8 * i + 8, :] = v
        w = inv_block[...]
        z[here, :] = dot3(split(w), split(z[here, :]), 1, 0)
        z[here, here] = w
        for jj in range(nb - 1):

            @pl.when(j == jj)
            def _():
                y = split(z[jj * B : jj * B + B, :])
                low = (jj + 1) * B
                z[low:, jj * B : low] = jnp.zeros((n - low, B), F32)
                for t in range(jj + 1, nb):
                    rows = slice(t * B, t * B + B)
                    z[rows, :] = z[rows, :] - dot3((y[0][:, rows], y[1][:, rows]), y, 0, 0)

        return carry

    lax.fori_loop(0, nb, body, 0)


def fill(dst, base, act, sig_cols, stat):
    a = act.astype(F32)
    for o in range(2):
        v = sig_cols[:, o : o + 1] * a
        v = (v - stat[2 * o : 2 * o + 1]) * stat[2 * o + 1 : 2 * o + 2]
        dst[base : base + ROWS, o * COLS : (o + 1) * COLS] = v.astype(BF)


def cols_of(rows):
    return jnp.transpose(rows)


def factor_kernel(
    a0, sig_all, stat_all, act, w_out, ar, ac, z, jac, sig_cols, inv_block, kbuf, sem, *sems
):
    q = pl.program_id(0)
    rest = Rest(act, ar, ac, kbuf, sems)
    pl.when(q == 0)(rest.begin)

    @pl.when(q == 0)
    def _():
        for h in range(2):
            sig_cols[h] = cols_of(sig_all[h])
        z[...] = jnp.zeros_like(z)

    for h in range(2):
        fill(jac, h * ROWS, a0[h, 0], sig_cols[h], stat_all[0])
    for r in range(WIDE // COLS):
        rows = slice(r * COLS, (r + 1) * COLS)
        z[rows, r * COLS :] += dot1(jac[rows, :], jac[r * COLS :, :])

    @pl.when(q == NP - 1)
    def _():
        for r in range(WIDE // B):
            rows = slice(r * B, (r + 1) * B)
            i = lax.broadcasted_iota(jnp.int32, (B, B), 0)
            j = lax.broadcasted_iota(jnp.int32, (B, B), 1)
            z[rows, rows] += jnp.where(i == j, DAMPING, 0.0).astype(F32)
        def between(j):
            pl.when(j == 1)(rest.second)
            pl.when(j == 8)(rest.third)

        factor_inverse(z, inv_block, between)
        copy = pltpu.make_async_copy(z, w_out, sem)
        copy.start()
        rest.end()
        copy.wait()


def factor(a0, sig_all, stat_all, act):
    dma = pltpu.SemaphoreType.DMA
    return pl.pallas_call(
        factor_kernel,
        name="factor",
        grid=(NP,),
        out_shape=(
            jax.ShapeDtypeStruct((WIDE, WIDE), F32),
            jax.ShapeDtypeStruct((NP, ROWS, COLS), BF),
            jax.ShapeDtypeStruct((2, NP, ROWS, COLS), BF),
        ),
        in_specs=[
            pl.BlockSpec((2, 1, ROWS, COLS), lambda q: (0, q, 0, 0)),
            pl.BlockSpec((2, 8, ROWS), lambda q: (0, 0, 0)),
            pl.BlockSpec((1, 8, COLS), lambda q: (q, 0, 0)),
            VM,
        ],
        out_specs=(ANY, ANY, ANY),
        scratch_shapes=[
            pltpu.VMEM((WIDE, WIDE), F32),
            pltpu.VMEM((WIDE, 2 * COLS), BF),
            pltpu.VMEM((2, ROWS, 8), F32),
            pltpu.VMEM((B, B), F32),
            pltpu.VMEM((NP, ROWS, COLS), BF),
            dma, dma((3,)), *[dma((NP,))] * 8,
        ],
        compiler_params=pltpu.CompilerParams(
            collective_id=1, has_side_effects=True, vmem_limit_bytes=56 * 2**20
        ),
    )(a0, sig_all, stat_all, act)


def final_kernel(
    ar, ac, a0, sig_all, stat_all, w_all, gram, panel,
    lead, jr, jc, j0, sig_r, sig_c, sig_0, w, sem,
):
    q = pl.program_id(0)
    s, p = place()
    width = WIDE // NP

    fetch = pltpu.make_async_copy(
        w_all.at[pl.ds(pl.multiple_of(p * width, 8), width), :], w, sem
    )

    @pl.when(q == 0)
    def _():
        fetch.start()
        sig_r[...] = cols_of(sig_all[s])
        for h in range(2):
            sig_c[h] = cols_of(sig_all[2 * p + h])
            sig_0[h] = cols_of(sig_all[h])
        gram[...] = jnp.zeros_like(gram)
        lead[...] = jnp.zeros_like(lead)

    stat = stat_all[0]
    fill(jr, 0, ar[0], sig_r, stat)
    for h in range(2):
        fill(jc, h * ROWS, ac[h, 0], sig_c[h], stat)
        fill(j0, h * ROWS, a0[h, 0], sig_0[h], stat)
    gram[...] += dot1(jr[...], jc[...])
    lead[...] += dot1(jr[...], j0[...])

    @pl.when(q == NP - 1)
    def _():
        i = lax.broadcasted_iota(jnp.int32, (ROWS, WIDE), 0) + s * ROWS
        j = lax.broadcasted_iota(jnp.int32, (ROWS, WIDE), 1)
        gram[...] += jnp.where(i == j + p * WIDE, DAMPING, 0.0).astype(F32)
        g = lead[...] + jnp.where(i == j, DAMPING, 0.0).astype(F32)
        fetch.wait()
        wi = lax.broadcasted_iota(jnp.int32, (width, WIDE), 0) + p * width
        wj = lax.broadcasted_iota(jnp.int32, (width, WIDE), 1)
        low = jnp.where(wj <= wi, w[...], 0.0)
        out = dot3(split(g), split(low), 1, 1)
        skip = jnp.logical_and(s == 0, p >= NP // 2)
        panel[...] = jnp.where(skip, 0.0, out)


def finish(ar, ac, a0, sig_all, stat_all, w_all):
    whole = lambda *shape: pl.BlockSpec(shape, lambda q: (0,) * len(shape))
    return pl.pallas_call(
        final_kernel,
        name="finish",
        grid=(NP,),
        out_shape=(
            jax.ShapeDtypeStruct((ROWS, WIDE), F32),
            jax.ShapeDtypeStruct((ROWS, WIDE // NP), F32),
        ),
        in_specs=[
            pl.BlockSpec((1, ROWS, COLS), lambda q: (q, 0, 0)),
            pl.BlockSpec((2, 1, ROWS, COLS), lambda q: (0, q, 0, 0)),
            pl.BlockSpec((2, 1, ROWS, COLS), lambda q: (0, q, 0, 0)),
            whole(NS, 8, ROWS),
            pl.BlockSpec((1, 8, COLS), lambda q: (q, 0, 0)),
            ANY,
        ],
        out_specs=(whole(ROWS, WIDE), whole(ROWS, WIDE // NP)),
        scratch_shapes=[
            pltpu.VMEM((ROWS, WIDE), F32),
            pltpu.VMEM((ROWS, 2 * COLS), BF),
            pltpu.VMEM((WIDE, 2 * COLS), BF),
            pltpu.VMEM((WIDE, 2 * COLS), BF),
            pltpu.VMEM((ROWS, 8), F32),
            pltpu.VMEM((2, ROWS, 8), F32),
            pltpu.VMEM((2, ROWS, 8), F32),
            pltpu.VMEM((WIDE // NP, WIDE), F32),
            pltpu.SemaphoreType.DMA,
        ],
        compiler_params=pltpu.CompilerParams(vmem_limit_bytes=56 * 2**20),
    )(ar, ac, a0, sig_all, stat_all, w_all)


def per_device(activations, signal):
    sig = signal.astype(F32)
    sig_rows = jnp.pad(sig.T, ((0, 6), (0, 0)))
    a0, sig_all, stat_all = gather_first(activations, sig, sig_rows)
    w, ar, ac = factor(a0, sig_all, stat_all, activations)
    return finish(ar, ac, a0, sig_all, stat_all, w)


def solution(mesh):
    return jax.shard_map(
        per_device,
        mesh=mesh,
        in_specs=(P("samp", "par"), P("samp", None)),
        out_specs=(P("samp", "par"), P("samp", "par")),
        check_vma=False,
    )
```

```python
import functools

import jax
import jax.numpy as jnp
from jax import lax
from jax.experimental import pallas as pl
from jax.experimental.pallas import tpu as pltpu
from jax.sharding import PartitionSpec as P

DAMPING = 0.5
EPSILON = 1e-05
F32 = jnp.float32
BF = jnp.bfloat16
MESH = pl.DeviceIdType.MESH
ANY = pl.BlockSpec(memory_space=pl.ANY)
VM = pl.BlockSpec(memory_space=pltpu.VMEM)

NX, NY, NZ = 4, 4, 2
NP = 8
NS = 16
ROWS = 640
COLS = 256
WIDE = 2 * ROWS
CH = 4
BCH = 2
NB = 10
B = 128


def place():
    s, p = lax.axis_index("samp"), lax.axis_index("par")
    return s, p


class Copies:
    def __init__(self):
        self.sent = []

    def send(self, src, dst, send_sem, recv_sem, s, p, cond=None):
        copy = pltpu.make_async_remote_copy(
            src_ref=src,
            dst_ref=dst,
            send_sem=send_sem,
            recv_sem=recv_sem,
            device_id={"samp": s, "par": p},
            device_id_type=MESH,
        )
        if cond is None:
            copy.start()
        else:
            pl.when(cond)(copy.start)
        self.sent.append((cond, copy))

    def drain(self):
        for cond, copy in self.sent:
            if cond is None:
                copy.wait_send()
            else:
                pl.when(cond)(copy.wait_send)


def arrived(ref, sem):
    pltpu.make_async_copy(ref, ref, sem).wait()


def split(v):
    hi = v.astype(BF)
    return hi, (v - hi.astype(F32)).astype(BF)


def dot3(a, b, ca, cb):
    dims = (((ca,), (cb,)), ((), ()))

    def one(u, v):
        return lax.dot_general(u, v, dims, preferred_element_type=F32)

    return one(a[0], b[1]) + one(a[1], b[0]) + one(a[0], b[0])


def dot1(a, b):
    return lax.dot_general(a, b, (((1,), (1,)), ((), ())), preferred_element_type=F32)


def row(v, i):
    return jnp.broadcast_to(v[i : i + 1, :], (8, B))


def lane(v, i):
    return jnp.broadcast_to(v[:, i : i + 1], (8, B))


def leaf(tiles, eye, sub):
    out = []
    for m in range(len(tiles)):
        top, unit = tiles[m], eye[m]
        cols = [[lane(tiles[i], 8 * m + b) for b in range(8)] for i in range(m, len(tiles))]
        scale, factors = None, []
        for k in range(8):
            r = lax.rsqrt(row(cols[0][k], k))
            inv = r * r
            scale = r if scale is None else jnp.where(sub == k, r, scale)
            pivots = [row(cols[0][k], b) for b in range(k + 1, 8)]
            f = [v[k] * inv for v in cols]
            for v, g in zip(cols, f):
                for b in range(k + 1, 8):
                    v[b] = v[b] - g * pivots[b - k - 1]
            if k < 7:
                below = jnp.where(sub > k, f[0], 0.0)
                top = top - below * row(top, k)
                unit = unit - below * row(unit, k)
            factors.append(f[1:])
        for n, i in enumerate(range(m + 1, len(tiles))):
            da = functools.reduce(jnp.add, [factors[k][n] * row(top, k) for k in range(8)])
            du = functools.reduce(jnp.add, [factors[k][n] * row(unit, k) for k in range(8)])
            tiles[i] = tiles[i] - da
            eye[i] = eye[i] - du
        out.append((unit * scale, top * scale))
    return out


def fill(dst, base, act, sig_cols, stat):
    a = act.astype(F32)
    for o in range(2):
        v = sig_cols[:, o : o + 1] * a
        v = (v - stat[2 * o : 2 * o + 1]) * stat[2 * o + 1 : 2 * o + 2]
        dst[base : base + ROWS, o * COLS : (o + 1) * COLS] = v.astype(BF)


def cols_of(rows):
    return jnp.transpose(rows)


def greet(s, p):
    c, k = lax.rem(s, 2), s // 2
    barrier = pltpu.get_barrier_semaphore()

    def signal(to_s, to_p):
        pl.semaphore_signal(
            barrier, inc=1, device_id={"samp": to_s, "par": to_p}, device_id_type=MESH
        )

    for i in range(1, NS):
        signal(lax.rem(s + i, NS), p)
    for i in range(1, NP):
        signal(s, lax.rem(p + i, NP))

    @pl.when(k != p)
    def _():
        signal(2 * p + c, k)

    pl.semaphore_wait(barrier, NS + NP - 2 + jnp.where(k == p, 0, 1))


class Place:
    def __init__(self):
        s, p = lax.axis_index("samp"), lax.axis_index("par")
        self.s, self.p = s, p
        self.c, self.k = lax.rem(s, 2), s // 2
        self.x, self.zh = lax.rem(self.k, NX), self.k // NX
        self.y, self.zl = p // NZ, lax.rem(p, NZ)
        self.other = s + 1 - 2 * self.c
        self.up, self.down = lax.rem(self.y + 1, NY), lax.rem(self.y + NY - 1, NY)
        self.far, self.lo = lax.rem(self.y + 2, NY), 1 - self.zl
        self.ahead = jnp.where(self.c == 0, self.up, self.down)
        self.behind = jnp.where(self.c == 0, self.down, self.up)
        self.relay = jnp.logical_or(
            jnp.logical_and(self.x == 1, self.c == 0), jnp.logical_and(self.x == 3, self.c == 1)
        )

    def samp_of(self, zz, xx):
        return 2 * (zz * NX + xx) + self.c

    def tree(self):
        return [
            (self.samp_of(self.zh, 1), self.x == 0),
            (self.samp_of(self.zh, 3), self.x == 0),
            (self.samp_of(1, 0), self.k == 0),
            (self.samp_of(self.zh, 2), self.relay),
        ]


def par_gather(here, net, buf, slot, pieces, sems, own, core, between):
    two_send, two_recv, core_send, core_recv = sems
    s, p, y, zl = here.s, here.p, here.y, here.zl
    up, down, far, lo = here.up, here.down, here.far, here.lo
    step = ROWS // pieces

    def par_of(yy, ll):
        return yy * NZ + ll

    def part(q, t):
        return buf.at[slot, q, pl.ds(t * step, step), :]

    def pass_on(q, t, i, to):
        net.send(part(q, t), part(q, t), two_send.at[i, t], two_recv.at[i, t], s, to)

    def across(q, t, i):
        net.send(part(q, t), part(q, t), core_send.at[i, t], core_recv.at[i, t], here.other, p, core)

    def stage_own(t):
        own(part(p, t), t)
        pass_on(p, t, 1, par_of(up, zl))
        pass_on(p, t, 2, par_of(down, zl))
        pass_on(p, t, 0, par_of(y, lo))
        across(p, t, 0)

    def stage_near(t):
        q = par_of(y, lo)
        arrived(part(q, t), two_recv.at[0, t])
        pass_on(q, t, 3, par_of(up, zl))
        pass_on(q, t, 4, par_of(down, zl))
        across(q, t, 1)
        qu, qd = par_of(down, zl), par_of(up, zl)
        arrived(part(qu, t), two_recv.at[1, t])
        arrived(part(qd, t), two_recv.at[2, t])
        pass_on(par_of(here.behind, zl), t, 5, par_of(here.ahead, zl))
        across(qu, t, 2)
        across(qd, t, 3)

    def stage_far(t):
        q = par_of(far, zl)
        arrived(part(q, t), two_recv.at[5, t])
        pass_on(q, t, 6, par_of(y, lo))
        across(q, t, 4)
        qu, qd = par_of(down, lo), par_of(up, lo)
        arrived(part(qu, t), two_recv.at[3, t])
        arrived(part(qd, t), two_recv.at[4, t])
        across(qu, t, 5)
        across(qd, t, 6)

    def stage_last(t):
        q = par_of(far, lo)
        arrived(part(q, t), two_recv.at[6, t])
        across(q, t, 7)

    for t in range(pieces + 3):
        for lag, stage in enumerate((stage_own, stage_near, stage_far, stage_last)):
            if 0 <= t - lag < pieces:
                stage(t - lag)
        between(t)

    def from_core():
        order = [
            (y, zl), (y, lo), (down, zl), (up, zl), (far, zl), (down, lo), (up, lo), (far, lo),
        ]
        for t in range(pieces):
            for i, (yy, ll) in enumerate(order):
                other = buf.at[1 - here.c, par_of(yy, ll), pl.ds(t * step, step), :]
                arrived(other, core_recv.at[i, t])

    return from_core


def own_sums(act, sig):
    def add(i, sums):
        rows = pl.ds(pl.multiple_of(i * 80, 80), 80)
        a = act[rows, :].astype(F32)
        g = sig[rows, :]
        new = []
        for o in range(2):
            v = g[:, o : o + 1] * a
            new.append(sums[2 * o] + jnp.sum(v.reshape(10, 8, COLS), axis=0))
            new.append(sums[2 * o + 1] + jnp.sum((v * v).reshape(10, 8, COLS), axis=0))
        return tuple(new)

    zero = jnp.zeros((8, COLS), F32)
    sums = lax.fori_loop(0, ROWS // 80, add, (zero,) * 4)
    return jnp.concatenate(
        [jnp.sum(v, axis=0, keepdims=True) for v in sums] + [jnp.zeros((4, COLS), F32)], axis=0
    )


def statistics(total):
    count, width = float(NS * ROWS), float(2 * COLS * NP)
    rows = []
    for o in range(2):
        average = total[2 * o : 2 * o + 1] / count
        second = total[2 * o + 1 : 2 * o + 2] / count
        rows += [average, 1.0 / jnp.sqrt(width * (second - average * average + EPSILON))]
    return jnp.concatenate(rows + [jnp.zeros((4, COLS), F32)], axis=0)


def factor_step(j, uu, diag, sub, ln):
    j0 = pl.multiple_of(j * B, B)
    here = pl.ds(j0, B)
    tiles = [uu[pl.ds(pl.multiple_of(j0 + 8 * i, 8), 8), here] for i in range(B // 8)]
    eye = [jnp.where(ln == sub + 8 * i, 1.0, 0.0).astype(F32) for i in range(B // 8)]
    for i, (w, u) in enumerate(leaf(tiles, eye, sub)):
        rows = pl.ds(pl.multiple_of(j0 + 8 * i, 8), 8)
        uu[rows, here] = w
        diag[rows, :] = u


def mega_kernel(
    act, sig, sig_rows, gram, panel,
    blk, ac, uu, lead, diag, jr, jw, mom, moms, sigs, stat, stats, sig_r, sig_c, sig_0,
    own_sem, a_two_send, a_two_recv, a_core_send, a_core_recv,
    b_two_send, b_two_recv, b_core_send, b_core_recv, one_send, one_recv,
    t_send, t_recv, col_send, col_recv, core_send, core_recv,
    u_send, u_recv, u_core_send, u_core_recv,
    mom_send, mom_recv, sig_send, sig_recv, stat_send, stat_recv,
):
    here = Place()
    s, p, c, k = here.s, here.p, here.c, here.k
    own_slot = jnp.where(k == 0, c, 2)
    net = Copies()
    first = pltpu.make_async_copy(act, blk.at[own_slot, p], own_sem.at[0])
    first.start()
    turn = pltpu.make_async_copy(act, ac.at[c, k], own_sem.at[1])

    @pl.when(k == p)
    def _():
        turn.start()

    greet(s, p)
    first.wait()

    def turn_away(cond):
        net.send(act, ac.at[c, p], t_send, t_recv, 2 * p + c, k, jnp.logical_and(cond, k != p))

    def no_wait(ref, t):
        pass

    def between(t):
        if t == 0:
            for i in range(1, NS):
                net.send(sig_rows, sigs.at[s], sig_send.at[i], sig_recv.at[s], lax.rem(s + i, NS), p)
            mom[...] = own_sums(act, sig)
            for i in range(1, NS):
                net.send(mom, moms.at[s], mom_send.at[i], mom_recv.at[s], lax.rem(s + i, NS), p)
            moms[s] = mom[...]
            sigs[s] = sig_rows[...]
            for i, (to, cond) in enumerate(here.tree()[:3]):
                for n in range(BCH):
                    ref = blk.at[c, p, pl.ds(n * (ROWS // BCH), ROWS // BCH), :]
                    net.send(ref, ref, one_send.at[i, n], one_recv.at[n], to, p, k == 0)
            turn_away(k > 0)
        if t == 1:
            for i in range(1, NS):
                j = lax.rem(s + i, NS)
                arrived(moms.at[j], mom_recv.at[j])
            total = moms[0]
            for j in range(1, NS):
                total = total + moms[j]
            stat[...] = statistics(total)
            for i in range(1, NP):
                net.send(stat, stats.at[p], stat_send.at[i], stat_recv.at[p], s, lax.rem(p + i, NP))
            stats[p] = stat[...]

    from_core = par_gather(
        here, net, blk, own_slot, CH, (a_two_send, a_two_recv, a_core_send, a_core_recv),
        no_wait, k == 0, between,
    )
    turn_away(k == 0)
    for i in range(1, NS):
        j = lax.rem(s + i, NS)
        arrived(sigs.at[j], sig_recv.at[j])
    for i in range(1, NP):
        j = lax.rem(p + i, NP)
        arrived(stats.at[j], stat_recv.at[j])
    sig_r[...] = cols_of(sigs[s])
    for h in range(2):
        sig_c[h] = cols_of(sigs[2 * p + h])
        sig_0[h] = cols_of(sigs[h])

    def columns_out():
        @pl.when(k == p)
        def _():
            turn.wait()

        @pl.when(k != p)
        def _():
            arrived(ac.at[c, k], t_recv)

        copies = []
        for i in range(1, NP):
            to = lax.rem(k + i, NP)
            copies.append(
                far_copy(ac.at[c, k], ac.at[c, k], col_send.at[i], col_recv.at[k], 2 * to + c, p)
            )
        copies.append(far_copy(ac.at[c, k], ac.at[c, k], core_send.at[0], core_recv.at[k], here.other, p))
        return copies

    def columns_across():
        copies = []
        for i in range(1, NP):
            j = lax.rem(k + i, NP)
            copies.append(far_copy(ac.at[c, j], ac.at[c, j], core_send.at[i], core_recv.at[j], here.other, p))
        return copies

    def start_across():
        for i, copy in enumerate(columns_across()):
            j = lax.rem(k + i + 1, NP)
            arrived(ac.at[c, j], col_recv.at[j])
            copy.start()

    def columns_done():
        for j in range(NP):
            arrived(ac.at[1 - c, j], core_recv.at[j])

    def own_gram():
        gram[...] = jnp.zeros_like(gram)

        def add(q, carry):
            fill(jr, 0, blk[own_slot, q], sig_r, stats[q])
            for h in range(2):
                fill(jw, h * ROWS, ac[h, q], sig_c[h], stats[q])
            gram[...] += dot1(jr[...], jw[...])
            return carry

        lax.fori_loop(0, NP, add, 0)
        i = lax.broadcasted_iota(jnp.int32, (ROWS, WIDE), 0) + s * ROWS
        j = lax.broadcasted_iota(jnp.int32, (ROWS, WIDE), 1) + p * WIDE
        gram[...] += jnp.where(i == j, DAMPING, 0.0).astype(F32)

    def u_rows(jj, half):
        return uu.at[pl.ds(jj * B + half * (B // 2), B // 2), jj * B :]

    def u_copies(jj):
        ref = u_rows(jj, c)
        return [
            (far_copy(ref, ref, u_send.at[i, jj], u_recv.at[jj], to, p), cond)
            for i, (to, cond) in enumerate(here.tree())
        ]

    def u_across(jj):
        ref = u_rows(jj, c)
        return far_copy(ref, ref, u_core_send.at[jj], u_core_recv.at[jj], here.other, p)

    @pl.when(k == 0)
    def _():
        from_core()
        uu[...] = jnp.zeros_like(uu)

        def add(q, carry):
            for h in range(2):
                fill(jw, h * ROWS, blk[h, q], sig_0[h], stats[q])
            for r in range(WIDE // COLS):
                rows = slice(r * COLS, (r + 1) * COLS)
                uu[rows, r * COLS :] += dot1(jw[rows, :], jw[r * COLS :, :])
            return carry

        lax.fori_loop(0, NP, add, 0)
        for copy in columns_out():
            copy.start()
        sub = lax.broadcasted_iota(jnp.int32, (8, B), 0)
        ln = lax.broadcasted_iota(jnp.int32, (8, B), 1)
        for r in range(NB):
            rows = slice(r * B, (r + 1) * B)
            i = lax.broadcasted_iota(jnp.int32, (B, B), 0)
            j = lax.broadcasted_iota(jnp.int32, (B, B), 1)
            uu[rows, rows] += jnp.where(i == j, DAMPING, 0.0).astype(F32)

        def body(j, carry):
            factor_step(j, uu, diag, sub, ln)
            for jj in range(NB):

                @pl.when(j == jj)
                def _():
                    rows = slice(jj * B, jj * B + B)
                    low = (jj + 1) * B
                    if jj < NB - 1:
                        x = dot3(split(uu[rows, rows]), split(uu[rows, low:]), 1, 0)
                        uu[rows, low:] = x
                        xs = split(x)
                    for copy, _ in u_copies(jj)[:3]:
                        copy.start()
                    for t in range(jj + 1, NB):
                        at = t * B - low
                        left = (xs[0][:, at : at + B], xs[1][:, at : at + B])
                        right = (xs[0][:, at:], xs[1][:, at:])
                        uu[t * B : t * B + B, t * B :] -= dot3(left, right, 0, 0)
                    if jj == 6:
                        start_across()

            return carry

        lax.fori_loop(0, NB, body, 0)
        columns_done()
        own_gram()
        for jj in range(NB):
            for copy, _ in u_copies(jj)[:3]:
                copy.wait_send()
        for j in range(NB):
            uu[j * B : j * B + B, j * B : j * B + B] = diag[j * B : j * B + B, :]
        width = WIDE // NP
        m = uu[pl.ds(pl.multiple_of(p * width, 8), width), pl.ds(pl.multiple_of(s * ROWS, B), ROWS)]
        i = lax.broadcasted_iota(jnp.int32, (width, ROWS), 0) + p * width
        j = lax.broadcasted_iota(jnp.int32, (width, ROWS), 1) + s * ROWS
        panel[...] = jnp.transpose(jnp.where(i <= j, m, 0.0))

    @pl.when(k > 0)
    def _():
        inner = Copies()
        for copy in columns_out():
            copy.start()

        def own(ref, t):
            arrived(ref, one_recv.at[t])
            for i, (to, cond) in enumerate(here.tree()):
                if i != 2:
                    inner.send(ref, ref, one_send.at[i, t], one_recv.at[t], to, p, cond)

        come = par_gather(
            here, inner, blk, c, BCH, (b_two_send, b_two_recv, b_core_send, b_core_recv),
            own, None, lambda t: None,
        )
        start_across()
        come()
        lead[...] = jnp.zeros_like(lead)

        def add(q, carry):
            fill(jr, 0, blk[2, q], sig_r, stats[q])
            for h in range(2):
                fill(jw, h * ROWS, blk[h, q], sig_0[h], stats[q])
            lead[...] += dot1(jr[...], jw[...])
            return carry

        lax.fori_loop(0, NP, add, 0)
        columns_done()
        own_gram()
        for jj in range(NB):
            arrived(u_rows(jj, c), u_recv.at[jj])
            for i, (copy, cond) in enumerate(u_copies(jj)):
                if i != 2:
                    pl.when(cond)(copy.start)
            u_across(jj).start()
            arrived(u_rows(jj, 1 - c), u_core_recv.at[jj])
            rows = slice(jj * B, jj * B + B)
            done = dot3(split(lead[:, rows]), split(uu[rows, rows]), 1, 1)
            lead[:, rows] = done
            if jj < NB - 1:
                halves = split(done)

                def minus(t, carry):
                    at = pl.ds(pl.multiple_of(t * B, B), B)
                    lead[:, at] -= dot3(halves, split(uu[rows, at]), 1, 0)
                    return carry

                lax.fori_loop(jj + 1, NB, minus, 0)
        width = WIDE // NP
        for pp in range(NP):

            @pl.when(p == pp)
            def _():
                panel[...] = lead[:, pp * width : (pp + 1) * width]

        for jj in range(NB):
            for i, (copy, cond) in enumerate(u_copies(jj)):
                if i != 2:
                    pl.when(cond)(copy.wait_send)
            u_across(jj).wait_send()
        inner.drain()

    for copy in columns_sent(here, ac, col_send, col_recv, core_send, core_recv):
        copy.wait_send()
    net.drain()


def columns_sent(here, ac, col_send, col_recv, core_send, core_recv):
    c, k, p = here.c, here.k, here.p
    copies = []
    for i in range(1, NP):
        to = lax.rem(k + i, NP)
        copies.append(far_copy(ac.at[c, k], ac.at[c, k], col_send.at[i], col_recv.at[k], 2 * to + c, p))
    for i in range(NP):
        j = lax.rem(k + i, NP)
        copies.append(far_copy(ac.at[c, j], ac.at[c, j], core_send.at[i], core_recv.at[j], here.other, p))
    return copies


def far_copy(src, dst, send_sem, recv_sem, s, p):
    return pltpu.make_async_remote_copy(
        src_ref=src,
        dst_ref=dst,
        send_sem=send_sem,
        recv_sem=recv_sem,
        device_id={"samp": s, "par": p},
        device_id_type=MESH,
    )


def per_device(activations, signal):
    sig = signal.astype(F32)
    sig_rows = jnp.pad(sig.T, ((0, 6), (0, 0)))
    dma, vm = pltpu.SemaphoreType.DMA, pltpu.VMEM
    return pl.pallas_call(
        mega_kernel,
        name="gram_and_panels",
        out_shape=(
            jax.ShapeDtypeStruct((ROWS, WIDE), F32),
            jax.ShapeDtypeStruct((ROWS, WIDE // NP), F32),
        ),
        in_specs=[VM, VM, VM],
        out_specs=(VM, VM),
        scratch_shapes=[
            vm((3, NP, ROWS, COLS), BF),
            vm((2, NP, ROWS, COLS), BF),
            vm((WIDE, WIDE), F32),
            vm((ROWS, WIDE), F32),
            vm((WIDE, B), F32),
            vm((ROWS, 2 * COLS), BF),
            vm((WIDE, 2 * COLS), BF),
            vm((8, COLS), F32),
            vm((NS, 8, COLS), F32),
            vm((NS, 8, ROWS), F32),
            vm((8, COLS), F32),
            vm((NP, 8, COLS), F32),
            vm((ROWS, 8), F32),
            vm((2, ROWS, 8), F32),
            vm((2, ROWS, 8), F32),
            dma((2,)),
            dma((7, CH)), dma((7, CH)), dma((8, CH)), dma((8, CH)),
            dma((7, BCH)), dma((7, BCH)), dma((8, BCH)), dma((8, BCH)), dma((4, BCH)), dma((BCH,)),
            dma, dma, dma((NP,)), dma((NP,)), dma((NP,)), dma((NP,)),
            dma((4, NB)), dma((NB,)), dma((NB,)), dma((NB,)),
            dma((NS,)), dma((NS,)), dma((NS,)), dma((NS,)), dma((NP,)), dma((NP,)),
        ],
        compiler_params=pltpu.CompilerParams(
            collective_id=0, has_side_effects=True, vmem_limit_bytes=60 * 2**20
        ),
    )(activations, sig, sig_rows)


def solution(mesh):
    return jax.shard_map(
        per_device,
        mesh=mesh,
        in_specs=(P("samp", "par"), P("samp", None)),
        out_specs=(P("samp", "par"), P("samp", "par")),
        check_vma=False,
    )
```

```python
import functools

import jax
import jax.numpy as jnp
from jax import lax
from jax.experimental import pallas as pl
from jax.experimental.pallas import tpu as pltpu
from jax.sharding import PartitionSpec as P

DAMPING = 0.5
EPSILON = 1e-05
F32 = jnp.float32
BF = jnp.bfloat16
MESH = pl.DeviceIdType.MESH
ANY = pl.BlockSpec(memory_space=pl.ANY)
VM = pl.BlockSpec(memory_space=pltpu.VMEM)

NX, NY, NZ = 4, 4, 2
NP = 8
NS = 16
ROWS = 640
COLS = 256
WIDE = 2 * ROWS
CH = 4
BCH = 2
NB = 10
B = 128


def place():
    s, p = lax.axis_index("samp"), lax.axis_index("par")
    return s, p


class Copies:
    def __init__(self):
        self.sent = []

    def send(self, src, dst, send_sem, recv_sem, s, p, cond=None):
        copy = pltpu.make_async_remote_copy(
            src_ref=src,
            dst_ref=dst,
            send_sem=send_sem,
            recv_sem=recv_sem,
            device_id={"samp": s, "par": p},
            device_id_type=MESH,
        )
        if cond is None:
            copy.start()
        else:
            pl.when(cond)(copy.start)
        self.sent.append((cond, copy))

    def drain(self):
        for cond, copy in self.sent:
            if cond is None:
                copy.wait_send()
            else:
                pl.when(cond)(copy.wait_send)


def arrived(ref, sem):
    pltpu.make_async_copy(ref, ref, sem).wait()


def split(v):
    hi = v.astype(BF)
    return hi, (v - hi.astype(F32)).astype(BF)


def dot3(a, b, ca, cb):
    dims = (((ca,), (cb,)), ((), ()))

    def one(u, v):
        return lax.dot_general(u, v, dims, preferred_element_type=F32)

    return one(a[0], b[1]) + one(a[1], b[0]) + one(a[0], b[0])


def dot1(a, b):
    return lax.dot_general(a, b, (((1,), (1,)), ((), ())), preferred_element_type=F32)


def row(v, i):
    return jnp.broadcast_to(v[i : i + 1, :], (8, B))


def lane(v, i):
    return jnp.broadcast_to(v[:, i : i + 1], (8, B))


def leaf(tiles, eye, sub):
    out = []
    for m in range(len(tiles)):
        top, unit = tiles[m], eye[m]
        cols = [[lane(tiles[i], 8 * m + b) for b in range(8)] for i in range(m, len(tiles))]
        scale, factors = None, []
        for k in range(8):
            r = lax.rsqrt(row(cols[0][k], k))
            inv = r * r
            scale = r if scale is None else jnp.where(sub == k, r, scale)
            pivots = [row(cols[0][k], b) for b in range(k + 1, 8)]
            f = [v[k] * inv for v in cols]
            for v, g in zip(cols, f):
                for b in range(k + 1, 8):
                    v[b] = v[b] - g * pivots[b - k - 1]
            if k < 7:
                below = jnp.where(sub > k, f[0], 0.0)
                top = top - below * row(top, k)
                unit = unit - below * row(unit, k)
            factors.append(f[1:])
        for n, i in enumerate(range(m + 1, len(tiles))):
            da = functools.reduce(jnp.add, [factors[k][n] * row(top, k) for k in range(8)])
            du = functools.reduce(jnp.add, [factors[k][n] * row(unit, k) for k in range(8)])
            tiles[i] = tiles[i] - da
            eye[i] = eye[i] - du
        out.append((unit * scale, top * scale))
    return out


def fill(dst, base, act, sig_cols, stat):
    a = act.astype(F32)
    for o in range(2):
        v = sig_cols[:, o : o + 1] * a
        v = (v - stat[2 * o : 2 * o + 1]) * stat[2 * o + 1 : 2 * o + 2]
        dst[base : base + ROWS, o * COLS : (o + 1) * COLS] = v.astype(BF)


def cols_of(rows):
    return jnp.transpose(rows)


def greet(s, p):
    c, k = lax.rem(s, 2), s // 2
    barrier = pltpu.get_barrier_semaphore()

    def signal(to_s, to_p):
        pl.semaphore_signal(
            barrier, inc=1, device_id={"samp": to_s, "par": to_p}, device_id_type=MESH
        )

    for i in range(1, NS):
        signal(lax.rem(s + i, NS), p)
    for i in range(1, NP):
        signal(s, lax.rem(p + i, NP))

    @pl.when(k != p)
    def _():
        signal(2 * p + c, k)

    pl.semaphore_wait(barrier, NS + NP - 2 + jnp.where(k == p, 0, 1))


class Place:
    def __init__(self):
        s, p = lax.axis_index("samp"), lax.axis_index("par")
        self.s, self.p = s, p
        self.c, self.k = lax.rem(s, 2), s // 2
        self.x, self.zh = lax.rem(self.k, NX), self.k // NX
        self.y, self.zl = p // NZ, lax.rem(p, NZ)
        self.other = s + 1 - 2 * self.c
        self.relay = jnp.logical_or(
            jnp.logical_and(self.x == 1, self.c == 0), jnp.logical_and(self.x == 3, self.c == 1)
        )

    def samp_of(self, zz, xx):
        return 2 * (zz * NX + xx) + self.c

    def tree(self):
        return [
            (self.samp_of(self.zh, 1), self.x == 0),
            (self.samp_of(self.zh, 3), self.x == 0),
            (self.samp_of(1, 0), self.k == 0),
            (self.samp_of(self.zh, 2), self.relay),
        ]


class Gather:
    def __init__(self, here, buf, index, ring, pair, where, pieces, sems, core=True, by_ring=False):
        self.here, self.buf, self.index = here, buf, index
        self.ring, self.pair, self.where = ring, pair, where
        self.up, self.down = lax.rem(ring + 1, 4), lax.rem(ring + 3, 4)
        self.far, self.lo = lax.rem(ring + 2, 4), 1 - pair
        self.ahead = jnp.where(here.c == 0, self.up, self.down)
        self.behind = jnp.where(here.c == 0, self.down, self.up)
        self.pieces, self.step, self.sems = pieces, ROWS // pieces, sems
        self.core, self.by_ring = core, by_ring

    def part(self, r, q, t, other=False):
        slot, _, _ = self.where(r, q)
        index = 1 - self.index if other else self.index
        return self.buf.at[index, slot, pl.ds(t * self.step, self.step), :]

    def wait(self, r, q, t, i):
        return ("wait", self.part(r, q, t), self.sems[1].at[i, t])

    def send(self, r, q, t, i, to_r, to_q):
        _, to_s, to_p = self.where(to_r, to_q)
        ref = self.part(r, q, t)
        copy = far_copy(ref, ref, self.sems[0].at[i, t], self.sems[1].at[i, t], to_s, to_p)
        return ("send", copy, None)

    def across(self, r, q, t, i):
        ref, here = self.part(r, q, t), self.here
        copy = far_copy(ref, ref, self.sems[2].at[i, t], self.sems[3].at[i, t], here.other, here.p)
        return ("send", copy, None if self.core is True else self.core)

    def events(self, stage, t):
        r, q, up, down, far, lo = self.ring, self.pair, self.up, self.down, self.far, self.lo
        if stage == 0:
            return [
                self.send(r, q, t, 1, up, q),
                self.send(r, q, t, 2, down, q),
                self.send(r, q, t, 0, r, lo),
                self.across(r, q, t, 0),
            ]
        if stage == 1:
            return [
                self.wait(r, lo, t, 0),
                self.send(r, lo, t, 3, up, q),
                self.send(r, lo, t, 4, down, q),
                self.across(r, lo, t, 1),
                self.wait(down, q, t, 1),
                self.wait(up, q, t, 2),
                self.send(self.behind, q, t, 5, self.ahead, q),
                self.across(down, q, t, 2),
                self.across(up, q, t, 3),
            ]
        if stage == 2:
            hand_on = [self.send(far, q, t, 6, r, lo)]
            relayed = [self.send(self.behind, lo, t, 6, self.ahead, q)]
            return [
                self.wait(far, q, t, 5),
                *([] if self.by_ring else hand_on),
                self.across(far, q, t, 4),
                self.wait(down, lo, t, 3),
                self.wait(up, lo, t, 4),
                *(relayed if self.by_ring else []),
                self.across(down, lo, t, 5),
                self.across(up, lo, t, 6),
            ]
        return [self.wait(far, lo, t, 6), self.across(far, lo, t, 7)]

    def run(self, stage, t):
        for event in self.events(stage, t):
            if event[0] == "wait":
                arrived(*event[1:])
            elif event[2] is None:
                event[1].start()
            else:
                pl.when(event[2])(event[1].start)

    def run_all(self, stage):
        for t in range(self.pieces):
            self.run(stage, t)

    def from_core(self):
        r, q, up, down, far, lo = self.ring, self.pair, self.up, self.down, self.far, self.lo
        order = [(r, q), (r, lo), (down, q), (up, q), (far, q), (down, lo), (up, lo), (far, lo)]
        for t in range(self.pieces):
            for i, (a, b) in enumerate(order):
                arrived(self.part(a, b, t, other=True), self.sems[3].at[i, t])

    def drain(self):
        for stage in range(4):
            for t in range(self.pieces):
                for kind, copy, cond in self.events(stage, t):
                    if kind == "send":
                        if cond is None:
                            copy.wait_send()
                        else:
                            pl.when(cond)(copy.wait_send)


def own_sums(act, sig):
    def add(i, sums):
        rows = pl.ds(pl.multiple_of(i * 80, 80), 80)
        a = act[rows, :].astype(F32)
        g = sig[rows, :]
        new = []
        for o in range(2):
            v = g[:, o : o + 1] * a
            new.append(sums[2 * o] + jnp.sum(v.reshape(10, 8, COLS), axis=0))
            new.append(sums[2 * o + 1] + jnp.sum((v * v).reshape(10, 8, COLS), axis=0))
        return tuple(new)

    zero = jnp.zeros((8, COLS), F32)
    sums = lax.fori_loop(0, ROWS // 80, add, (zero,) * 4)
    return jnp.concatenate(
        [jnp.sum(v, axis=0, keepdims=True) for v in sums] + [jnp.zeros((4, COLS), F32)], axis=0
    )


def statistics(total):
    count, width = float(NS * ROWS), float(2 * COLS * NP)
    rows = []
    for o in range(2):
        average = total[2 * o : 2 * o + 1] / count
        second = total[2 * o + 1 : 2 * o + 2] / count
        rows += [average, 1.0 / jnp.sqrt(width * (second - average * average + EPSILON))]
    return jnp.concatenate(rows + [jnp.zeros((4, COLS), F32)], axis=0)


def factor_step(j, uu, diag, sub, ln):
    j0 = pl.multiple_of(j * B, B)
    here = pl.ds(j0, B)
    tiles = [uu[pl.ds(pl.multiple_of(j0 + 8 * i, 8), 8), here] for i in range(B // 8)]
    eye = [jnp.where(ln == sub + 8 * i, 1.0, 0.0).astype(F32) for i in range(B // 8)]
    for i, (w, u) in enumerate(leaf(tiles, eye, sub)):
        rows = pl.ds(pl.multiple_of(j0 + 8 * i, 8), 8)
        uu[rows, here] = w
        diag[rows, :] = u


def mega_kernel(
    act, sig, gram, panel,
    blk, ac, uu, lead, diag, jr, jw, mom, moms, sigs, stat, stats, sig_own, sig_r, sig_c, sig_0,
    own_sem, a_two_send, a_two_recv, a_core_send, a_core_recv,
    b_two_send, b_two_recv, b_core_send, b_core_recv,
    c_two_send, c_two_recv, c_core_send, c_core_recv, one_send, one_recv,
    t_send, t_recv, u_send, u_recv, u_core_send, u_core_recv,
    mom_send, mom_recv, sig_send, sig_recv, stat_send, stat_recv,
):
    here = Place()
    s, p, c, k = here.s, here.p, here.c, here.k
    own_slot = jnp.where(k == 0, c, 2)
    net = Copies()
    first = pltpu.make_async_copy(act, blk.at[own_slot, p], own_sem.at[0])
    first.start()
    turn = pltpu.make_async_copy(act, ac.at[c, k], own_sem.at[1])

    @pl.when(k == p)
    def _():
        turn.start()

    sig_own[...] = jnp.concatenate([sig[...].astype(F32), jnp.zeros((6, ROWS), F32)], axis=0)
    sigs[s] = sig_own[...]
    sig_r[...] = cols_of(sig_own[...])
    greet(s, p)
    first.wait()

    def on_par(r, q):
        return r * NZ + q, s, r * NZ + q

    def on_samp(r, q):
        return q * NX + r, here.samp_of(q, r), p

    rows_in = Gather(
        here, blk, own_slot, here.y, here.zl, on_par, CH,
        (a_two_send, a_two_recv, a_core_send, a_core_recv), core=k == 0,
    )
    lead_in = Gather(
        here, blk, c, here.y, here.zl, on_par, BCH,
        (b_two_send, b_two_recv, b_core_send, b_core_recv),
    )
    cols_in = Gather(
        here, ac, c, here.x, here.zh, on_samp, BCH,
        (c_two_send, c_two_recv, c_core_send, c_core_recv), by_ring=True,
    )

    def turn_away(cond):
        net.send(act, ac.at[c, p], t_send, t_recv, 2 * p + c, k, jnp.logical_and(cond, k != p))

    def turned():
        @pl.when(k == p)
        def _():
            turn.wait()

        @pl.when(k != p)
        def _():
            arrived(ac.at[c, k], t_recv)

    for t in range(CH + 3):
        for stage in range(4):
            if 0 <= t - stage < CH:
                rows_in.run(stage, t - stage)
        if t == 0:
            for i, (to, cond) in enumerate(here.tree()[:3]):
                for n in range(BCH):
                    ref = lead_in.part(here.y, here.zl, n)
                    net.send(ref, ref, one_send.at[i, n], one_recv.at[n], to, p, k == 0)
            mom[...] = own_sums(act, sig_r)
            for i in range(1, NS):
                net.send(mom, moms.at[s], mom_send.at[i], mom_recv.at[s], lax.rem(s + i, NS), p)
            moms[s] = mom[...]
        if t == 1:
            for i in range(1, NS):
                net.send(sig_own, sigs.at[s], sig_send.at[i], sig_recv.at[s], lax.rem(s + i, NS), p)
            turn_away(k > 0)
        if t == 3:
            for i in range(1, NS):
                j = lax.rem(s + i, NS)
                arrived(moms.at[j], mom_recv.at[j])
            total = moms[0]
            for j in range(1, NS):
                total = total + moms[j]
            stat[...] = statistics(total)
            for i in range(1, NP):
                net.send(stat, stats.at[p], stat_send.at[i], stat_recv.at[p], s, lax.rem(p + i, NP))
            stats[p] = stat[...]

    turn_away(k == 0)
    for i in range(1, NS):
        j = lax.rem(s + i, NS)
        arrived(sigs.at[j], sig_recv.at[j])
    for h in range(2):
        sig_c[h] = cols_of(sigs[2 * p + h])
        sig_0[h] = cols_of(sigs[h])
    for i in range(1, NP):
        j = lax.rem(p + i, NP)
        arrived(stats.at[j], stat_recv.at[j])

    def gram_part(start, stop):
        def add(q, carry):
            fill(jr, 0, blk[own_slot, q], sig_r, stats[q])
            for h in range(2):
                fill(jw, h * ROWS, ac[h, q], sig_c[h], stats[q])
            gram[...] += dot1(jr[...], jw[...])
            return carry

        lax.fori_loop(start, stop, add, 0)

    def gram_first():
        i = lax.broadcasted_iota(jnp.int32, (ROWS, WIDE), 0) + s * ROWS
        j = lax.broadcasted_iota(jnp.int32, (ROWS, WIDE), 1) + p * WIDE
        gram[...] = jnp.where(i == j, DAMPING, 0.0).astype(F32)

    def u_rows(jj, half):
        return uu.at[pl.ds(jj * B + half * (B // 2), B // 2), jj * B :]

    def u_copies(jj):
        ref = u_rows(jj, c)
        return [
            (far_copy(ref, ref, u_send.at[i, jj], u_recv.at[jj], to, p), cond)
            for i, (to, cond) in enumerate(here.tree())
        ]

    def u_across(jj):
        ref = u_rows(jj, c)
        return far_copy(ref, ref, u_core_send.at[jj], u_core_recv.at[jj], here.other, p)

    width = WIDE // NP
    own_cols = pl.ds(pl.multiple_of(p * width, 8), width)

    @pl.when(k == 0)
    def _():
        rows_in.from_core()
        uu[...] = jnp.zeros_like(uu)

        def add(q, carry):
            for h in range(2):
                fill(jw, h * ROWS, blk[h, q], sig_0[h], stats[q])
            for r in range(WIDE // COLS):
                rows = slice(r * COLS, (r + 1) * COLS)
                uu[rows, r * COLS :] += dot1(jw[rows, :], jw[r * COLS :, :])
            return carry

        lax.fori_loop(0, NP, add, 0)
        turned()
        cols_in.run_all(0)
        sub = lax.broadcasted_iota(jnp.int32, (8, B), 0)
        ln = lax.broadcasted_iota(jnp.int32, (8, B), 1)
        for r in range(NB):
            rows = slice(r * B, (r + 1) * B)
            i = lax.broadcasted_iota(jnp.int32, (B, B), 0)
            j = lax.broadcasted_iota(jnp.int32, (B, B), 1)
            uu[rows, rows] += jnp.where(i == j, DAMPING, 0.0).astype(F32)

        def body(j, carry):
            factor_step(j, uu, diag, sub, ln)
            for jj in range(NB):

                @pl.when(j == jj)
                def _():
                    rows = slice(jj * B, jj * B + B)
                    low = (jj + 1) * B
                    if jj < NB - 1:
                        x = dot3(split(uu[rows, rows]), split(uu[rows, low:]), 1, 0)
                        uu[rows, low:] = x
                        xs = split(x)
                    for copy, _ in u_copies(jj)[:3]:
                        copy.start()
                    for t in range(jj + 1, NB):
                        at = t * B - low
                        left = (xs[0][:, at : at + B], xs[1][:, at : at + B])
                        right = (xs[0][:, at:], xs[1][:, at:])
                        uu[t * B : t * B + B, t * B :] -= dot3(left, right, 0, 0)
                    if jj in (1, 3, 5):
                        cols_in.run_all((jj + 1) // 2)

            return carry

        lax.fori_loop(0, NB, body, 0)
        cols_in.from_core()
        gram_first()
        gram_part(0, NP)
        for jj in range(NB):
            for copy, _ in u_copies(jj)[:3]:
                copy.wait_send()
        for j in range(NB):
            uu[j * B : j * B + B, j * B : j * B + B] = diag[j * B : j * B + B, :]
        m = uu[own_cols, pl.ds(pl.multiple_of(s * ROWS, B), ROWS)]
        i = lax.broadcasted_iota(jnp.int32, (width, ROWS), 0) + p * width
        j = lax.broadcasted_iota(jnp.int32, (width, ROWS), 1) + s * ROWS
        panel[...] = jnp.where(i <= j, m, 0.0)

    @pl.when(k > 0)
    def _():
        inner = Copies()
        for t in range(BCH + 3):
            if t < BCH:
                ref = lead_in.part(here.y, here.zl, t)
                arrived(ref, one_recv.at[t])
                for i, (to, cond) in enumerate(here.tree()):
                    if i != 2:
                        inner.send(ref, ref, one_send.at[i, t], one_recv.at[t], to, p, cond)
            for stage in range(4):
                if 0 <= t - stage < BCH:
                    lead_in.run(stage, t - stage)
            if t == 1:
                turned()
                cols_in.run_all(0)
        lead_in.from_core()
        lead[...] = jnp.zeros_like(lead)

        def add(q, carry):
            fill(jr, 0, blk[2, q], sig_r, stats[q])
            for h in range(2):
                fill(jw, h * ROWS, blk[h, q], sig_0[h], stats[q])
            lead[...] += dot1(jw[...], jr[...])
            return carry

        cols_in.run_all(1)
        lax.fori_loop(0, NP // 2, add, 0)
        cols_in.run_all(2)
        lax.fori_loop(NP // 2, NP, add, 0)
        cols_in.run_all(3)
        gram_first()
        for jj in range(NB):
            if jj in (3, 6):
                if jj == 3:
                    cols_in.from_core()
                gram_part(0 if jj == 3 else NP // 2, NP // 2 if jj == 3 else NP)
            arrived(u_rows(jj, c), u_recv.at[jj])
            for i, (copy, cond) in enumerate(u_copies(jj)):
                if i != 2:
                    pl.when(cond)(copy.start)
            u_across(jj).start()
            arrived(u_rows(jj, 1 - c), u_core_recv.at[jj])
            rows = slice(jj * B, jj * B + B)
            done = dot3(split(uu[rows, rows]), split(lead[rows, :]), 1, 0)
            lead[rows, :] = done
            if jj < NB - 1:
                halves = split(done)

                def minus(t, carry):
                    at = pl.ds(pl.multiple_of(t * B, B), B)
                    lead[at, :] -= dot3(split(uu[rows, at]), halves, 0, 0)
                    return carry

                lax.fori_loop(jj + 1, NB, minus, 0)
        panel[...] = lead[own_cols, :]
        for jj in range(NB):
            for i, (copy, cond) in enumerate(u_copies(jj)):
                if i != 2:
                    pl.when(cond)(copy.wait_send)
            u_across(jj).wait_send()
        lead_in.drain()
        inner.drain()

    cols_in.drain()
    rows_in.drain()
    net.drain()


def far_copy(src, dst, send_sem, recv_sem, s, p):
    return pltpu.make_async_remote_copy(
        src_ref=src,
        dst_ref=dst,
        send_sem=send_sem,
        recv_sem=recv_sem,
        device_id={"samp": s, "par": p},
        device_id_type=MESH,
    )


def per_device(activations, signal):
    dma, vm = pltpu.SemaphoreType.DMA, pltpu.VMEM

    def gather_sems(pieces):
        return [dma((7, pieces)), dma((7, pieces)), dma((8, pieces)), dma((8, pieces))]

    gram, panel = pl.pallas_call(
        mega_kernel,
        name="gram_and_panels",
        out_shape=(
            jax.ShapeDtypeStruct((ROWS, WIDE), F32),
            jax.ShapeDtypeStruct((WIDE // NP, ROWS), F32),
        ),
        in_specs=[VM, VM],
        out_specs=(VM, VM),
        scratch_shapes=[
            vm((3, NP, ROWS, COLS), BF),
            vm((2, NP, ROWS, COLS), BF),
            vm((WIDE, WIDE), F32),
            vm((WIDE, ROWS), F32),
            vm((WIDE, B), F32),
            vm((ROWS, 2 * COLS), BF),
            vm((WIDE, 2 * COLS), BF),
            vm((8, COLS), F32),
            vm((NS, 8, COLS), F32),
            vm((NS, 8, ROWS), F32),
            vm((8, COLS), F32),
            vm((NP, 8, COLS), F32),
            vm((8, ROWS), F32),
            vm((ROWS, 8), F32),
            vm((2, ROWS, 8), F32),
            vm((2, ROWS, 8), F32),
            dma((2,)),
            *gather_sems(CH), *gather_sems(BCH), *gather_sems(BCH),
            dma((4, BCH)), dma((BCH,)), dma, dma,
            dma((4, NB)), dma((NB,)), dma((NB,)), dma((NB,)),
            dma((NS,)), dma((NS,)), dma((NS,)), dma((NS,)), dma((NP,)), dma((NP,)),
        ],
        compiler_params=pltpu.CompilerParams(
            collective_id=0, has_side_effects=True, vmem_limit_bytes=60 * 2**20
        ),
    )(activations, signal.T)
    return gram, panel.T


def solution(mesh):
    return jax.shard_map(
        per_device,
        mesh=mesh,
        in_specs=(P("samp", "par"), P("samp", None)),
        out_specs=(P("samp", "par"), P("samp", "par")),
        check_vma=False,
    )
```

```python
import functools

import jax
import jax.numpy as jnp
from jax import lax
from jax.experimental import pallas as pl
from jax.experimental.pallas import tpu as pltpu
from jax.sharding import PartitionSpec as P

DAMPING = 0.5
EPSILON = 1e-05
F32 = jnp.float32
BF = jnp.bfloat16
MESH = pl.DeviceIdType.MESH
ANY = pl.BlockSpec(memory_space=pl.ANY)
VM = pl.BlockSpec(memory_space=pltpu.VMEM)

NX, NY, NZ = 4, 4, 2
NP = 8
NS = 16
ROWS = 640
COLS = 256
WIDE = 2 * ROWS
CH = 4
BCH = 2
NB = 10
B = 128


def place():
    s, p = lax.axis_index("samp"), lax.axis_index("par")
    return s, p


class Copies:
    def __init__(self):
        self.sent = []

    def send(self, src, dst, send_sem, recv_sem, s, p, cond=None):
        copy = pltpu.make_async_remote_copy(
            src_ref=src,
            dst_ref=dst,
            send_sem=send_sem,
            recv_sem=recv_sem,
            device_id={"samp": s, "par": p},
            device_id_type=MESH,
        )
        if cond is None:
            copy.start()
        else:
            pl.when(cond)(copy.start)
        self.sent.append((cond, copy))

    def drain(self):
        for cond, copy in self.sent:
            if cond is None:
                copy.wait_send()
            else:
                pl.when(cond)(copy.wait_send)


def arrived(ref, sem):
    pltpu.make_async_copy(ref, ref, sem).wait()


def split(v):
    hi = v.astype(BF)
    return hi, (v - hi.astype(F32)).astype(BF)


def dot3(a, b, ca, cb):
    dims = (((ca,), (cb,)), ((), ()))

    def one(u, v):
        return lax.dot_general(u, v, dims, preferred_element_type=F32)

    return one(a[0], b[1]) + one(a[1], b[0]) + one(a[0], b[0])


def dot1(a, b):
    return lax.dot_general(a, b, (((1,), (1,)), ((), ())), preferred_element_type=F32)


def row(v, i):
    return jnp.broadcast_to(v[i : i + 1, :], (8, B))


def lane(v, i):
    return jnp.broadcast_to(v[:, i : i + 1], (8, B))


def leaf(tiles, eye, sub):
    out = []
    for m in range(len(tiles)):
        top, unit = tiles[m], eye[m]
        cols = [[lane(tiles[i], 8 * m + b) for b in range(8)] for i in range(m, len(tiles))]
        scale, factors = None, []
        for k in range(8):
            r = lax.rsqrt(row(cols[0][k], k))
            inv = r * r
            scale = r if scale is None else jnp.where(sub == k, r, scale)
            pivots = [row(cols[0][k], b) for b in range(k + 1, 8)]
            f = [v[k] * inv for v in cols]
            for v, g in zip(cols, f):
                for b in range(k + 1, 8):
                    v[b] = v[b] - g * pivots[b - k - 1]
            if k < 7:
                below = jnp.where(sub > k, f[0], 0.0)
                top = top - below * row(top, k)
                unit = unit - below * row(unit, k)
            factors.append(f[1:])
        for n, i in enumerate(range(m + 1, len(tiles))):
            da = functools.reduce(jnp.add, [factors[k][n] * row(top, k) for k in range(8)])
            du = functools.reduce(jnp.add, [factors[k][n] * row(unit, k) for k in range(8)])
            tiles[i] = tiles[i] - da
            eye[i] = eye[i] - du
        out.append((unit * scale, top * scale))
    return out


def fill(dst, base, act, sig_cols, stat):
    a = act.astype(F32)
    for o in range(2):
        v = sig_cols[:, o : o + 1] * a
        v = (v - stat[2 * o : 2 * o + 1]) * stat[2 * o + 1 : 2 * o + 2]
        dst[base : base + ROWS, o * COLS : (o + 1) * COLS] = v.astype(BF)


def cols_of(rows):
    return jnp.transpose(jnp.concatenate([rows.astype(F32), jnp.zeros((6, ROWS), F32)], axis=0))


def greet(s, p):
    c, k = lax.rem(s, 2), s // 2
    barrier = pltpu.get_barrier_semaphore()

    def signal(to_s, to_p):
        pl.semaphore_signal(
            barrier, inc=1, device_id={"samp": to_s, "par": to_p}, device_id_type=MESH
        )

    for i in range(1, NS):
        signal(lax.rem(s + i, NS), p)
    for i in range(1, NP):
        signal(s, lax.rem(p + i, NP))

    @pl.when(k != p)
    def _():
        signal(2 * p + c, k)

    pl.semaphore_wait(barrier, NS + NP - 2 + jnp.where(k == p, 0, 1))


class Place:
    def __init__(self):
        s, p = lax.axis_index("samp"), lax.axis_index("par")
        self.s, self.p = s, p
        self.c, self.k = lax.rem(s, 2), s // 2
        self.x, self.zh = lax.rem(self.k, NX), self.k // NX
        self.y, self.zl = p // NZ, lax.rem(p, NZ)
        self.other = s + 1 - 2 * self.c
    def samp_of(self, zz, xx):
        return 2 * (zz * NX + xx) + self.c

    def tree(self):
        x, zh, c = self.x, self.zh, self.c
        root = jnp.where(zh == 0, 0, c)
        turn = lax.rem(x - root + NX, NX)
        side = jnp.where(c == 0, turn == 1, turn == 3)
        return [
            (self.samp_of(zh, lax.rem(root + 1, NX)), turn == 0),
            (self.samp_of(zh, lax.rem(root + 3, NX)), turn == 0),
            (self.samp_of(1, x), jnp.logical_and(zh == 0, x == c)),
            (self.samp_of(zh, lax.rem(root + 2, NX)), side),
        ]

    def level(self):
        root = jnp.where(self.zh == 0, 0, self.c)
        turn = lax.rem(self.x - root + NX, NX)
        return jnp.where(self.zh == 0, 0, 1 + self.c) + jnp.where(turn == 2, 2, jnp.where(turn == 0, 0, 1))


class Gather:
    def __init__(self, here, buf, index, ring, pair, where, pieces, sems, core=True, by_ring=False, busy=None):
        self.here, self.buf, self.index = here, buf, index
        self.ring, self.pair, self.where = ring, pair, where
        self.up, self.down = lax.rem(ring + 1, 4), lax.rem(ring + 3, 4)
        self.far, self.lo = lax.rem(ring + 2, 4), 1 - pair
        self.ahead = jnp.where(here.c == 0, self.up, self.down)
        self.behind = jnp.where(here.c == 0, self.down, self.up)
        self.pieces, self.step, self.sems = pieces, ROWS // pieces, sems
        self.core, self.by_ring, self.busy = core, by_ring, busy

    def part(self, r, q, t, other=False):
        slot, _, _ = self.where(r, q)
        index = 1 - self.index if other else self.index
        return self.buf.at[index, slot, pl.ds(t * self.step, self.step), :]

    def wait(self, r, q, t, i):
        return ("wait", self.part(r, q, t), self.sems[1].at[i, t])

    def send(self, r, q, t, i, to_r, to_q):
        _, to_s, to_p = self.where(to_r, to_q)
        ref = self.part(r, q, t)
        copy = far_copy(ref, ref, self.sems[0].at[i, t], self.sems[1].at[i, t], to_s, to_p)
        return ("send", copy, None)

    def relay(self, *args):
        kind, copy, _ = self.send(*args)
        return (kind, copy, None if self.busy is None else jnp.logical_not(self.busy))

    def direct(self, t):
        if self.busy is None:
            return []
        r, q, c = self.ring, self.pair, self.here.c
        end = jnp.where(r == 3, 1, 3)
        side = jnp.where(c == 0, r == 3, r == 1)
        ref = self.part(r, q, t)
        found = []
        for n, (i, to, cond) in enumerate((
            (3, 1, jnp.logical_and(r == 0, q == 1)),
            (4, 3, jnp.logical_and(r == 0, q == 1)),
            (5, end, jnp.logical_and(side, q == 0)),
            (6, end, jnp.logical_and(side, q == 1)),
        )):
            _, to_s, to_p = self.where(to, 0)
            copy = far_copy(ref, ref, self.sems[0].at[7 + n, t], self.sems[1].at[i, t], to_s, to_p)
            found.append(("send", copy, cond))
        return found

    def across(self, r, q, t, i):
        ref, here = self.part(r, q, t), self.here
        copy = far_copy(ref, ref, self.sems[2].at[i, t], self.sems[3].at[i, t], here.other, here.p)
        return ("send", copy, None if self.core is True else self.core)

    def events(self, stage, t):
        r, q, up, down, far, lo = self.ring, self.pair, self.up, self.down, self.far, self.lo
        if stage == 0:
            return [
                self.send(r, q, t, 1, up, q),
                self.send(r, q, t, 2, down, q),
                self.send(r, q, t, 0, r, lo),
                self.across(r, q, t, 0),
                *self.direct(t),
            ]
        if stage == 1:
            return [
                self.wait(r, lo, t, 0),
                self.relay(r, lo, t, 3, up, q),
                self.relay(r, lo, t, 4, down, q),
                self.across(r, lo, t, 1),
                self.wait(down, q, t, 1),
                self.wait(up, q, t, 2),
                self.relay(self.behind, q, t, 5, self.ahead, q),
                self.across(down, q, t, 2),
                self.across(up, q, t, 3),
            ]
        if stage == 2:
            hand_on = [self.relay(far, q, t, 6, r, lo)]
            relayed = [self.relay(self.behind, lo, t, 6, self.ahead, q)]
            return [
                self.wait(far, q, t, 5),
                *([] if self.by_ring else hand_on),
                self.across(far, q, t, 4),
                self.wait(down, lo, t, 3),
                self.wait(up, lo, t, 4),
                *(relayed if self.by_ring else []),
                self.across(down, lo, t, 5),
                self.across(up, lo, t, 6),
            ]
        return [self.wait(far, lo, t, 6), self.across(far, lo, t, 7)]

    def run(self, stage, t):
        for event in self.events(stage, t):
            if event[0] == "wait":
                arrived(*event[1:])
            elif event[2] is None:
                event[1].start()
            else:
                pl.when(event[2])(event[1].start)

    def run_all(self, stage):
        for t in range(self.pieces):
            self.run(stage, t)

    def from_core(self):
        r, q, up, down, far, lo = self.ring, self.pair, self.up, self.down, self.far, self.lo
        order = [(r, q), (r, lo), (down, q), (up, q), (far, q), (down, lo), (up, lo), (far, lo)]
        for t in range(self.pieces):
            for i, (a, b) in enumerate(order):
                arrived(self.part(a, b, t, other=True), self.sems[3].at[i, t])

    def drain(self):
        for stage in range(4):
            for t in range(self.pieces):
                for kind, copy, cond in self.events(stage, t):
                    if kind == "send":
                        if cond is None:
                            copy.wait_send()
                        else:
                            pl.when(cond)(copy.wait_send)


def own_sums(act, sig):
    def add(i, sums):
        rows = pl.ds(pl.multiple_of(i * 80, 80), 80)
        a = act[rows, :].astype(F32)
        g = sig[rows, :]
        new = []
        for o in range(2):
            v = g[:, o : o + 1] * a
            new.append(sums[2 * o] + jnp.sum(v.reshape(10, 8, COLS), axis=0))
            new.append(sums[2 * o + 1] + jnp.sum((v * v).reshape(10, 8, COLS), axis=0))
        return tuple(new)

    zero = jnp.zeros((8, COLS), F32)
    sums = lax.fori_loop(0, ROWS // 80, add, (zero,) * 4)
    return jnp.concatenate(
        [jnp.sum(v, axis=0, keepdims=True) for v in sums] + [jnp.zeros((4, COLS), F32)], axis=0
    )


def statistics(total):
    count, width = float(NS * ROWS), float(2 * COLS * NP)
    rows = []
    for o in range(2):
        average = total[2 * o : 2 * o + 1] / count
        second = total[2 * o + 1 : 2 * o + 2] / count
        rows += [average, 1.0 / jnp.sqrt(width * (second - average * average + EPSILON))]
    return jnp.concatenate(rows + [jnp.zeros((4, COLS), F32)], axis=0)


def factor_step(j, uu, diag, sub, ln):
    j0 = pl.multiple_of(j * B, B)
    here = pl.ds(j0, B)
    tiles = [uu[pl.ds(pl.multiple_of(j0 + 8 * i, 8), 8), here] for i in range(B // 8)]
    eye = [jnp.where(ln == sub + 8 * i, 1.0, 0.0).astype(F32) for i in range(B // 8)]
    for i, (w, u) in enumerate(leaf(tiles, eye, sub)):
        rows = pl.ds(pl.multiple_of(j0 + 8 * i, 8), 8)
        uu[rows, here] = w
        diag[rows, :] = u


def mega_kernel(
    act, sig, gram, panel,
    blk, ac, uu, lead, diag, jr, jw, mom, moms, sigs, stat, stats, sig_r, sig_c, sig_0,
    own_sem, a_two_send, a_two_recv, a_core_send, a_core_recv,
    b_two_send, b_two_recv, b_core_send, b_core_recv,
    c_two_send, c_two_recv, c_core_send, c_core_recv, one_send, one_recv,
    t_send, t_recv, u_send, u_recv, u_core_send, u_core_recv,
    mom_send, mom_recv, sig_send, sig_recv, stat_send, stat_recv,
):
    here = Place()
    s, p, c, k = here.s, here.p, here.c, here.k
    own_slot = jnp.where(k == 0, c, 2)
    net = Copies()
    first = pltpu.make_async_copy(act, blk.at[own_slot, p], own_sem.at[0])
    first.start()
    turn = pltpu.make_async_copy(act, ac.at[c, k], own_sem.at[1])

    @pl.when(k == p)
    def _():
        turn.start()

    sigs[s] = sig[...]
    sig_r[...] = cols_of(sig[...])
    greet(s, p)
    first.wait()

    def on_par(r, q):
        return r * NZ + q, s, r * NZ + q

    def on_samp(r, q):
        return q * NX + r, here.samp_of(q, r), p

    rows_in = Gather(
        here, blk, own_slot, here.y, here.zl, on_par, CH,
        (a_two_send, a_two_recv, a_core_send, a_core_recv), core=k == 0,
    )
    lead_in = Gather(
        here, blk, c, here.y, here.zl, on_par, BCH,
        (b_two_send, b_two_recv, b_core_send, b_core_recv),
    )
    cols_in = Gather(
        here, ac, c, here.x, here.zh, on_samp, BCH,
        (c_two_send, c_two_recv, c_core_send, c_core_recv), by_ring=True, busy=k == 0,
    )

    def turn_away(cond):
        net.send(act, ac.at[c, p], t_send, t_recv, 2 * p + c, k, jnp.logical_and(cond, k != p))

    def turned():
        @pl.when(k == p)
        def _():
            turn.wait()

        @pl.when(k != p)
        def _():
            arrived(ac.at[c, k], t_recv)

    level = here.level()

    def set_out(copies, when, only):
        for n in range(BCH) if only is None else [only]:
            ref = lead_in.part(here.y, here.zl, n)
            for i, (to, cond) in enumerate(here.tree()):
                copies.send(ref, ref, one_send.at[i, n], one_recv.at[n], to, p, jnp.logical_and(when, cond))

    def set_in(n):
        arrived(lead_in.part(here.y, here.zl, n), one_recv.at[n])

    for t in range(CH + 3):
        for stage in range(4):
            if 0 <= t - stage < CH:
                rows_in.run(stage, t - stage)
        if t == 0:
            set_out(net, k == 0, None)
            wanted = jnp.logical_or(k == 0, k == p)
            for i in range(1, NS):
                to = lax.rem(s + i, NS)
                net.send(sig, sigs.at[s], sig_send.at[i], sig_recv.at[s], to, p, wanted)
            mom[...] = own_sums(act, sig_r)
            for i in range(1, NS):
                net.send(mom, moms.at[s], mom_send.at[i], mom_recv.at[s], lax.rem(s + i, NS), p)
            moms[s] = mom[...]
        if t == 1:
            turn_away(k > 0)
        if t == 3:
            for i in range(1, NS):
                j = lax.rem(s + i, NS)
                arrived(moms.at[j], mom_recv.at[j])
            total = moms[0]
            for j in range(1, NS):
                total = total + moms[j]
            stat[...] = statistics(total)
            for i in range(1, NP):
                net.send(stat, stats.at[p], stat_send.at[i], stat_recv.at[p], s, lax.rem(p + i, NP))
            stats[p] = stat[...]

    turn_away(k == 0)

    @pl.when(level == 1)
    def _():
        for n in range(BCH):
            set_in(n)

    set_out(net, level == 1, None)
    for h in range(2):
        for j, cond in ((h, s != h), (2 * p + h, jnp.logical_and(p > 0, s != 2 * p + h))):
            pl.when(cond)(functools.partial(arrived, sigs.at[j], sig_recv.at[j]))
    for h in range(2):
        sig_c[h] = cols_of(sigs[2 * p + h])
        sig_0[h] = cols_of(sigs[h])
    for i in range(1, NP):
        j = lax.rem(p + i, NP)
        arrived(stats.at[j], stat_recv.at[j])

    def gram_part(start, stop):
        def add(q, carry):
            fill(jr, 0, blk[own_slot, q], sig_r, stats[q])
            for h in range(2):
                fill(jw, h * ROWS, ac[h, q], sig_c[h], stats[q])
            gram[...] += dot1(jr[...], jw[...])
            return carry

        lax.fori_loop(start, stop, add, 0)

    def gram_first():
        i = lax.broadcasted_iota(jnp.int32, (ROWS, WIDE), 0) + s * ROWS
        j = lax.broadcasted_iota(jnp.int32, (ROWS, WIDE), 1) + p * WIDE
        gram[...] = jnp.where(i == j, DAMPING, 0.0).astype(F32)

    def u_rows(jj, half):
        return uu.at[pl.ds(jj * B + half * (B // 2), B // 2), jj * B :]

    def u_copies(jj):
        ref = u_rows(jj, c)
        return [
            (far_copy(ref, ref, u_send.at[i, jj], u_recv.at[jj], to, p), cond)
            for i, (to, cond) in enumerate(here.tree())
        ]

    def u_across(jj):
        ref = u_rows(jj, c)
        return far_copy(ref, ref, u_core_send.at[jj], u_core_recv.at[jj], here.other, p)

    width = WIDE // NP
    own_cols = pl.ds(pl.multiple_of(p * width, 8), width)

    @pl.when(k == 0)
    def _():
        rows_in.from_core()
        uu[...] = jnp.zeros_like(uu)

        def add(q, carry):
            for h in range(2):
                fill(jw, h * ROWS, blk[h, q], sig_0[h], stats[q])
            for r in range(WIDE // COLS):
                rows = slice(r * COLS, (r + 1) * COLS)
                uu[rows, r * COLS :] += dot1(jw[rows, :], jw[r * COLS :, :])
            return carry

        lax.fori_loop(0, NP, add, 0)
        turned()
        cols_in.run_all(0)
        sub = lax.broadcasted_iota(jnp.int32, (8, B), 0)
        ln = lax.broadcasted_iota(jnp.int32, (8, B), 1)
        for r in range(NB):
            rows = slice(r * B, (r + 1) * B)
            i = lax.broadcasted_iota(jnp.int32, (B, B), 0)
            j = lax.broadcasted_iota(jnp.int32, (B, B), 1)
            uu[rows, rows] += jnp.where(i == j, DAMPING, 0.0).astype(F32)

        def body(j, carry):
            factor_step(j, uu, diag, sub, ln)
            for jj in range(NB):

                @pl.when(j == jj)
                def _():
                    rows = slice(jj * B, jj * B + B)
                    low = (jj + 1) * B
                    if jj < NB - 1:
                        x = dot3(split(uu[rows, rows]), split(uu[rows, low:]), 1, 0)
                        uu[rows, low:] = x
                        xs = split(x)
                    for copy, cond in u_copies(jj):
                        pl.when(cond)(copy.start)
                    for t in range(jj + 1, NB):
                        at = t * B - low
                        left = (xs[0][:, at : at + B], xs[1][:, at : at + B])
                        right = (xs[0][:, at:], xs[1][:, at:])
                        uu[t * B : t * B + B, t * B :] -= dot3(left, right, 0, 0)

            return carry

        lax.fori_loop(0, NB, body, 0)
        for stage in (1, 2, 3):
            cols_in.run_all(stage)
        gram_first()
        cols_in.from_core()
        gram_part(0, NP)
        for jj in range(NB):
            for copy, cond in u_copies(jj):
                pl.when(cond)(copy.wait_send)
        for j in range(NB):
            uu[j * B : j * B + B, j * B : j * B + B] = diag[j * B : j * B + B, :]
        m = uu[own_cols, pl.ds(pl.multiple_of(s * ROWS, B), ROWS)]
        i = lax.broadcasted_iota(jnp.int32, (width, ROWS), 0) + p * width
        j = lax.broadcasted_iota(jnp.int32, (width, ROWS), 1) + s * ROWS
        panel[...] = jnp.where(i <= j, m, 0.0)

    @pl.when(k > 0)
    def _():
        inner = Copies()
        for t in range(BCH + 3):
            if t < BCH:
                pl.when(level > 1)(functools.partial(set_in, t))
                set_out(inner, level > 1, t)
            for stage in range(4):
                if 0 <= t - stage < BCH:
                    lead_in.run(stage, t - stage)
            if t == 1:
                turned()
                cols_in.run_all(0)
            if t == 3:
                cols_in.run_all(1)
        cols_in.run_all(2)
        lead_in.from_core()
        lead[...] = jnp.zeros_like(lead)

        def add(q, carry):
            fill(jr, 0, blk[2, q], sig_r, stats[q])
            for h in range(2):
                fill(jw, h * ROWS, blk[h, q], sig_0[h], stats[q])
            lead[...] += dot1(jw[...], jr[...])
            return carry

        groups = ((0, 1, 2), (3,), (4,), (5, 6), (7,), (8,), (9,))

        def pass_on(jj):
            arrived(u_rows(jj, c), u_recv.at[jj])
            for copy, cond in u_copies(jj):
                pl.when(cond)(copy.start)
            u_across(jj).start()

        def pass_groups(r):
            for depth in range(4):
                if 0 <= r - depth < len(groups):

                    @pl.when(level == depth + 1)
                    def _():
                        for jj in groups[r - depth]:
                            pass_on(jj)

        def substitute(r):
            for jj in groups[r]:
                arrived(u_rows(jj, 1 - c), u_core_recv.at[jj])
                rows = slice(jj * B, jj * B + B)
                done = dot3(split(uu[rows, rows]), split(lead[rows, :]), 1, 0)
                lead[rows, :] = done
                if jj < NB - 1:
                    low = (jj + 1) * B
                    lead[low:, :] -= dot3(split(uu[rows, low:]), split(done), 0, 0)

        pass_groups(0)
        lax.fori_loop(0, NP // 2, add, 0)
        pass_groups(1)
        cols_in.run_all(3)
        lax.fori_loop(NP // 2, NP, add, 0)
        pass_groups(2)
        gram_first()
        cols_in.from_core()
        gram_part(0, NP // 2)
        pass_groups(3)
        substitute(0)
        pass_groups(4)
        substitute(1)
        gram_part(NP // 2, NP)
        for r in range(5, 10):
            pass_groups(r)
            substitute(r - 3)
        panel[...] = lead[own_cols, :]
        for jj in range(NB):
            for copy, cond in u_copies(jj):
                pl.when(cond)(copy.wait_send)
            u_across(jj).wait_send()
        lead_in.drain()
        inner.drain()

    cols_in.drain()
    rows_in.drain()
    net.drain()


def far_copy(src, dst, send_sem, recv_sem, s, p):
    return pltpu.make_async_remote_copy(
        src_ref=src,
        dst_ref=dst,
        send_sem=send_sem,
        recv_sem=recv_sem,
        device_id={"samp": s, "par": p},
        device_id_type=MESH,
    )


def per_device(activations, signal):
    dma, vm = pltpu.SemaphoreType.DMA, pltpu.VMEM

    def gather_sems(pieces):
        return [dma((11, pieces)), dma((7, pieces)), dma((8, pieces)), dma((8, pieces))]

    gram, panel = pl.pallas_call(
        mega_kernel,
        name="gram_and_panels",
        out_shape=(
            jax.ShapeDtypeStruct((ROWS, WIDE), F32),
            jax.ShapeDtypeStruct((WIDE // NP, ROWS), F32),
        ),
        in_specs=[VM, VM],
        out_specs=(VM, VM),
        scratch_shapes=[
            vm((3, NP, ROWS, COLS), BF),
            vm((2, NP, ROWS, COLS), BF),
            vm((WIDE, WIDE), F32),
            vm((WIDE, ROWS), F32),
            vm((WIDE, B), F32),
            vm((ROWS, 2 * COLS), BF),
            vm((WIDE, 2 * COLS), BF),
            vm((8, COLS), F32),
            vm((NS, 8, COLS), F32),
            vm((NS, 2, ROWS), BF),
            vm((8, COLS), F32),
            vm((NP, 8, COLS), F32),
            vm((ROWS, 8), F32),
            vm((2, ROWS, 8), F32),
            vm((2, ROWS, 8), F32),
            dma((2,)),
            *gather_sems(CH), *gather_sems(BCH), *gather_sems(BCH),
            dma((4, BCH)), dma((BCH,)), dma, dma,
            dma((4, NB)), dma((NB,)), dma((NB,)), dma((NB,)),
            dma((NS,)), dma((NS,)), dma((NS,)), dma((NS,)), dma((NP,)), dma((NP,)),
        ],
        compiler_params=pltpu.CompilerParams(
            collective_id=0, has_side_effects=True, vmem_limit_bytes=60 * 2**20
        ),
    )(activations, signal.T)
    return gram, panel.T


def solution(mesh):
    return jax.shard_map(
        per_device,
        mesh=mesh,
        in_specs=(P("samp", "par"), P("samp", None)),
        out_specs=(P("samp", "par"), P("samp", "par")),
        check_vma=False,
    )
```

```python
import functools

import jax
import jax.numpy as jnp
from jax import lax
from jax.experimental import pallas as pl
from jax.experimental.pallas import tpu as pltpu
from jax.sharding import PartitionSpec as P

DAMPING = 0.5
EPSILON = 1e-05
F32 = jnp.float32
BF = jnp.bfloat16
MESH = pl.DeviceIdType.MESH
ANY = pl.BlockSpec(memory_space=pl.ANY)
VM = pl.BlockSpec(memory_space=pltpu.VMEM)

NX, NY, NZ = 4, 4, 2
NP = 8
NS = 16
ROWS = 640
COLS = 256
WIDE = 2 * ROWS
CH = 4
BCH = 2
NB = 10
B = 128


def place():
    s, p = lax.axis_index("samp"), lax.axis_index("par")
    return s, p


class Copies:
    def __init__(self):
        self.sent = []

    def send(self, src, dst, send_sem, recv_sem, s, p, cond=None):
        copy = pltpu.make_async_remote_copy(
            src_ref=src,
            dst_ref=dst,
            send_sem=send_sem,
            recv_sem=recv_sem,
            device_id={"samp": s, "par": p},
            device_id_type=MESH,
        )
        if cond is None:
            copy.start()
        else:
            pl.when(cond)(copy.start)
        self.sent.append((cond, copy))

    def drain(self):
        for cond, copy in self.sent:
            if cond is None:
                copy.wait_send()
            else:
                pl.when(cond)(copy.wait_send)


def arrived(ref, sem):
    pltpu.make_async_copy(ref, ref, sem).wait()


def split(v):
    hi = v.astype(BF)
    return hi, (v - hi.astype(F32)).astype(BF)


def dot3(a, b, ca, cb):
    dims = (((ca,), (cb,)), ((), ()))

    def one(u, v):
        return lax.dot_general(u, v, dims, preferred_element_type=F32)

    return one(a[0], b[1]) + one(a[1], b[0]) + one(a[0], b[0])


def dot1(a, b):
    return lax.dot_general(a, b, (((1,), (1,)), ((), ())), preferred_element_type=F32)


def row(v, i):
    return jnp.broadcast_to(v[i : i + 1, :], (8, B))


def lane(v, i):
    return jnp.broadcast_to(v[:, i : i + 1], (8, B))


def leaf(tiles, eye, sub):
    out = []
    for m in range(len(tiles)):
        top, unit = tiles[m], eye[m]
        cols = [[lane(tiles[i], 8 * m + b) for b in range(8)] for i in range(m, len(tiles))]
        scale, factors = None, []
        for k in range(8):
            r = lax.rsqrt(row(cols[0][k], k))
            inv = r * r
            scale = r if scale is None else jnp.where(sub == k, r, scale)
            pivots = [row(cols[0][k], b) for b in range(k + 1, 8)]
            f = [v[k] * inv for v in cols]
            for v, g in zip(cols, f):
                for b in range(k + 1, 8):
                    v[b] = v[b] - g * pivots[b - k - 1]
            if k < 7:
                below = jnp.where(sub > k, f[0], 0.0)
                top = top - below * row(top, k)
                unit = unit - below * row(unit, k)
            factors.append(f[1:])
        for n, i in enumerate(range(m + 1, len(tiles))):
            da = functools.reduce(jnp.add, [factors[k][n] * row(top, k) for k in range(8)])
            du = functools.reduce(jnp.add, [factors[k][n] * row(unit, k) for k in range(8)])
            tiles[i] = tiles[i] - da
            eye[i] = eye[i] - du
        out.append((unit * scale, top * scale))
    return out


def fill(dst, base, act, sig_cols, stat):
    a = act.astype(F32)
    for o in range(2):
        v = sig_cols[:, o : o + 1] * a
        v = (v - stat[2 * o : 2 * o + 1]) * stat[2 * o + 1 : 2 * o + 2]
        dst[base : base + ROWS, o * COLS : (o + 1) * COLS] = v.astype(BF)


def cols_of(rows):
    return jnp.transpose(jnp.concatenate([rows.astype(F32), jnp.zeros((6, ROWS), F32)], axis=0))


def greet(s, p):
    c, k = lax.rem(s, 2), s // 2
    barrier = pltpu.get_barrier_semaphore()

    def signal(to_s, to_p):
        pl.semaphore_signal(
            barrier, inc=1, device_id={"samp": to_s, "par": to_p}, device_id_type=MESH
        )

    for i in range(1, NS):
        signal(lax.rem(s + i, NS), p)
    for i in range(1, NP):
        signal(s, lax.rem(p + i, NP))

    @pl.when(k != p)
    def _():
        signal(2 * p + c, k)

    pl.semaphore_wait(barrier, NS + NP - 2 + jnp.where(k == p, 0, 1))


class Place:
    def __init__(self):
        s, p = lax.axis_index("samp"), lax.axis_index("par")
        self.s, self.p = s, p
        self.c, self.k = lax.rem(s, 2), s // 2
        self.x, self.zh = lax.rem(self.k, NX), self.k // NX
        self.y, self.zl = p // NZ, lax.rem(p, NZ)
        self.other = s + 1 - 2 * self.c
    def samp_of(self, zz, xx):
        return 2 * (zz * NX + xx) + self.c

    def tree(self):
        x, zh, c = self.x, self.zh, self.c
        root = jnp.where(zh == 0, 0, c)
        turn = lax.rem(x - root + NX, NX)
        side = jnp.where(c == zh, turn == 1, turn == 3)
        return [
            (self.samp_of(zh, lax.rem(root + 1, NX)), turn == 0),
            (self.samp_of(zh, lax.rem(root + 3, NX)), turn == 0),
            (self.samp_of(1, x), jnp.logical_and(zh == 0, x == c)),
            (self.samp_of(zh, lax.rem(root + 2, NX)), side),
        ]

    def level(self):
        root = jnp.where(self.zh == 0, 0, self.c)
        turn = lax.rem(self.x - root + NX, NX)
        return jnp.where(self.zh == 0, 0, 1 + self.c) + jnp.where(turn == 2, 2, jnp.where(turn == 0, 0, 1))


class Gather:
    def __init__(self, here, buf, index, ring, pair, where, pieces, sems, core=True, by_ring=False, busy=None):
        self.here, self.buf, self.index = here, buf, index
        self.ring, self.pair, self.where = ring, pair, where
        self.up, self.down = lax.rem(ring + 1, 4), lax.rem(ring + 3, 4)
        self.far, self.lo = lax.rem(ring + 2, 4), 1 - pair
        self.ahead = jnp.where(here.c == 0, self.up, self.down)
        self.behind = jnp.where(here.c == 0, self.down, self.up)
        self.pieces, self.step, self.sems = pieces, ROWS // pieces, sems
        self.core, self.by_ring, self.busy = core, by_ring, busy

    def part(self, r, q, t, other=False):
        slot, _, _ = self.where(r, q)
        index = 1 - self.index if other else self.index
        return self.buf.at[index, slot, pl.ds(t * self.step, self.step), :]

    def wait(self, r, q, t, i):
        return ("wait", self.part(r, q, t), self.sems[1].at[i, t])

    def send(self, r, q, t, i, to_r, to_q):
        _, to_s, to_p = self.where(to_r, to_q)
        ref = self.part(r, q, t)
        copy = far_copy(ref, ref, self.sems[0].at[i, t], self.sems[1].at[i, t], to_s, to_p)
        return ("send", copy, None)

    def relay(self, *args):
        kind, copy, _ = self.send(*args)
        return (kind, copy, None if self.busy is None else jnp.logical_not(self.busy))

    def direct(self, t):
        if self.busy is None:
            return []
        r, q, c = self.ring, self.pair, self.here.c
        end = jnp.where(r == 3, 1, 3)
        side = jnp.where(c == 0, r == 3, r == 1)
        ref = self.part(r, q, t)
        found = []
        for n, (i, to, cond) in enumerate((
            (3, 1, jnp.logical_and(r == 0, q == 1)),
            (4, 3, jnp.logical_and(r == 0, q == 1)),
            (5, end, jnp.logical_and(side, q == 0)),
            (6, end, jnp.logical_and(side, q == 1)),
        )):
            _, to_s, to_p = self.where(to, 0)
            copy = far_copy(ref, ref, self.sems[0].at[7 + n, t], self.sems[1].at[i, t], to_s, to_p)
            found.append(("send", copy, cond))
        return found

    def across(self, r, q, t, i):
        ref, here = self.part(r, q, t), self.here
        copy = far_copy(ref, ref, self.sems[2].at[i, t], self.sems[3].at[i, t], here.other, here.p)
        return ("send", copy, None if self.core is True else self.core)

    def events(self, stage, t):
        r, q, up, down, far, lo = self.ring, self.pair, self.up, self.down, self.far, self.lo
        if stage == 0:
            return [
                self.send(r, q, t, 1, up, q),
                self.send(r, q, t, 2, down, q),
                self.send(r, q, t, 0, r, lo),
                self.across(r, q, t, 0),
                *self.direct(t),
            ]
        if stage == 1:
            return [
                self.wait(r, lo, t, 0),
                self.relay(r, lo, t, 3, up, q),
                self.relay(r, lo, t, 4, down, q),
                self.across(r, lo, t, 1),
                self.wait(down, q, t, 1),
                self.wait(up, q, t, 2),
                self.relay(self.behind, q, t, 5, self.ahead, q),
                self.across(down, q, t, 2),
                self.across(up, q, t, 3),
            ]
        if stage == 2:
            hand_on = [self.relay(far, q, t, 6, r, lo)]
            relayed = [self.relay(self.behind, lo, t, 6, self.ahead, q)]
            return [
                self.wait(far, q, t, 5),
                *([] if self.by_ring else hand_on),
                self.across(far, q, t, 4),
                self.wait(down, lo, t, 3),
                self.wait(up, lo, t, 4),
                *(relayed if self.by_ring else []),
                self.across(down, lo, t, 5),
                self.across(up, lo, t, 6),
            ]
        return [self.wait(far, lo, t, 6), self.across(far, lo, t, 7)]

    def run(self, stage, t):
        for event in self.events(stage, t):
            if event[0] == "wait":
                arrived(*event[1:])
            elif event[2] is None:
                event[1].start()
            else:
                pl.when(event[2])(event[1].start)

    def run_all(self, stage):
        for t in range(self.pieces):
            self.run(stage, t)

    def from_core(self):
        r, q, up, down, far, lo = self.ring, self.pair, self.up, self.down, self.far, self.lo
        order = [(r, q), (r, lo), (down, q), (up, q), (far, q), (down, lo), (up, lo), (far, lo)]
        for t in range(self.pieces):
            for i, (a, b) in enumerate(order):
                arrived(self.part(a, b, t, other=True), self.sems[3].at[i, t])

    def drain(self):
        for stage in range(4):
            for t in range(self.pieces):
                for kind, copy, cond in self.events(stage, t):
                    if kind == "send":
                        if cond is None:
                            copy.wait_send()
                        else:
                            pl.when(cond)(copy.wait_send)


def own_sums(act, sig):
    def add(i, sums):
        rows = pl.ds(pl.multiple_of(i * 80, 80), 80)
        a = act[rows, :].astype(F32)
        g = sig[rows, :]
        new = []
        for o in range(2):
            v = g[:, o : o + 1] * a
            new.append(sums[2 * o] + jnp.sum(v.reshape(10, 8, COLS), axis=0))
            new.append(sums[2 * o + 1] + jnp.sum((v * v).reshape(10, 8, COLS), axis=0))
        return tuple(new)

    zero = jnp.zeros((8, COLS), F32)
    sums = lax.fori_loop(0, ROWS // 80, add, (zero,) * 4)
    return jnp.concatenate(
        [jnp.sum(v, axis=0, keepdims=True) for v in sums] + [jnp.zeros((4, COLS), F32)], axis=0
    )


def statistics(total):
    count, width = float(NS * ROWS), float(2 * COLS * NP)
    rows = []
    for o in range(2):
        average = total[2 * o : 2 * o + 1] / count
        second = total[2 * o + 1 : 2 * o + 2] / count
        rows += [average, 1.0 / jnp.sqrt(width * (second - average * average + EPSILON))]
    return jnp.concatenate(rows + [jnp.zeros((4, COLS), F32)], axis=0)


def factor_step(j, uu, diag, sub, ln):
    j0 = pl.multiple_of(j * B, B)
    here = pl.ds(j0, B)
    tiles = [uu[pl.ds(pl.multiple_of(j0 + 8 * i, 8), 8), here] for i in range(B // 8)]
    eye = [jnp.where(ln == sub + 8 * i, 1.0, 0.0).astype(F32) for i in range(B // 8)]
    for i, (w, u) in enumerate(leaf(tiles, eye, sub)):
        rows = pl.ds(pl.multiple_of(j0 + 8 * i, 8), 8)
        uu[rows, here] = w
        diag[rows, :] = u


def mega_kernel(
    act, sig, gram, panel,
    blk, ac, uu, lead, diag, jr, jw, mom, moms, sigs, stat, stats, sig_r, sig_c, sig_0,
    own_sem, a_two_send, a_two_recv, a_core_send, a_core_recv,
    b_two_send, b_two_recv, b_core_send, b_core_recv,
    c_two_send, c_two_recv, c_core_send, c_core_recv, one_send, one_recv,
    t_send, t_recv, u_send, u_recv, u_core_send, u_core_recv,
    mom_send, mom_recv, sig_send, sig_recv, stat_send, stat_recv,
):
    here = Place()
    s, p, c, k = here.s, here.p, here.c, here.k
    own_slot = jnp.where(k == 0, c, 2)
    net = Copies()
    first = pltpu.make_async_copy(act, blk.at[own_slot, p], own_sem.at[0])
    first.start()
    turn = pltpu.make_async_copy(act, ac.at[c, k], own_sem.at[1])

    @pl.when(k == p)
    def _():
        turn.start()

    sigs[s] = sig[...]
    sig_r[...] = cols_of(sig[...])
    greet(s, p)
    first.wait()

    def on_par(r, q):
        return r * NZ + q, s, r * NZ + q

    def on_samp(r, q):
        return q * NX + r, here.samp_of(q, r), p

    rows_in = Gather(
        here, blk, own_slot, here.y, here.zl, on_par, CH,
        (a_two_send, a_two_recv, a_core_send, a_core_recv), core=k == 0,
    )
    lead_in = Gather(
        here, blk, c, here.y, here.zl, on_par, BCH,
        (b_two_send, b_two_recv, b_core_send, b_core_recv),
    )
    cols_in = Gather(
        here, ac, c, here.x, here.zh, on_samp, BCH,
        (c_two_send, c_two_recv, c_core_send, c_core_recv), by_ring=True, busy=k == 0,
    )

    def turned():
        @pl.when(k == p)
        def _():
            turn.wait()

        @pl.when(k != p)
        def _():
            arrived(ac.at[c, k], t_recv)

    level = here.level()

    def set_out(copies, when, only):
        for n in range(BCH) if only is None else [only]:
            ref = lead_in.part(here.y, here.zl, n)
            for i, (to, cond) in enumerate(here.tree()):
                copies.send(ref, ref, one_send.at[i, n], one_recv.at[n], to, p, jnp.logical_and(when, cond))

    def set_in(n):
        arrived(lead_in.part(here.y, here.zl, n), one_recv.at[n])

    for t in range(CH + 3):
        for stage in range(4):
            if 0 <= t - stage < CH:
                rows_in.run(stage, t - stage)
        if t == 0:
            set_out(net, k == 0, None)
            wanted = jnp.logical_or(k == 0, k == p)
            for i in range(1, NS):
                to = lax.rem(s + i, NS)
                net.send(sig, sigs.at[s], sig_send.at[i], sig_recv.at[s], to, p, wanted)
            mom[...] = own_sums(act, sig_r)
            for i in range(1, NS):
                net.send(mom, moms.at[s], mom_send.at[i], mom_recv.at[s], lax.rem(s + i, NS), p)
            moms[s] = mom[...]
        if t == 3:
            for i in range(1, NS):
                j = lax.rem(s + i, NS)
                arrived(moms.at[j], mom_recv.at[j])
            total = moms[0]
            for j in range(1, NS):
                total = total + moms[j]
            stat[...] = statistics(total)
            for i in range(1, NP):
                net.send(stat, stats.at[p], stat_send.at[i], stat_recv.at[p], s, lax.rem(p + i, NP))
            stats[p] = stat[...]

    net.send(act, ac.at[c, p], t_send, t_recv, 2 * p + c, k, k != p)

    @pl.when(level == 1)
    def _():
        for n in range(BCH):
            set_in(n)

    set_out(net, level == 1, None)
    for h in range(2):
        for j, cond in ((h, s != h), (2 * p + h, jnp.logical_and(p > 0, s != 2 * p + h))):
            pl.when(cond)(functools.partial(arrived, sigs.at[j], sig_recv.at[j]))
    for h in range(2):
        sig_c[h] = cols_of(sigs[2 * p + h])
        sig_0[h] = cols_of(sigs[h])
    for i in range(1, NP):
        j = lax.rem(p + i, NP)
        arrived(stats.at[j], stat_recv.at[j])

    def gram_part(start, stop):
        def add(q, carry):
            fill(jr, 0, blk[own_slot, q], sig_r, stats[q])
            for h in range(2):
                fill(jw, h * ROWS, ac[h, q], sig_c[h], stats[q])
            gram[...] += dot1(jr[...], jw[...])
            return carry

        lax.fori_loop(start, stop, add, 0)

    def gram_first():
        i = lax.broadcasted_iota(jnp.int32, (ROWS, WIDE), 0) + s * ROWS
        j = lax.broadcasted_iota(jnp.int32, (ROWS, WIDE), 1) + p * WIDE
        gram[...] = jnp.where(i == j, DAMPING, 0.0).astype(F32)

    def u_rows(jj, half):
        return uu.at[pl.ds(jj * B + half * (B // 2), B // 2), jj * B :]

    def u_copies(jj):
        ref = u_rows(jj, c)
        return [
            (far_copy(ref, ref, u_send.at[i, jj], u_recv.at[jj], to, p), cond)
            for i, (to, cond) in enumerate(here.tree())
        ]

    def u_across(jj):
        ref = u_rows(jj, c)
        return far_copy(ref, ref, u_core_send.at[jj], u_core_recv.at[jj], here.other, p)

    width = WIDE // NP
    own_cols = pl.ds(pl.multiple_of(p * width, 8), width)

    @pl.when(k == 0)
    def _():
        rows_in.from_core()
        uu[...] = jnp.zeros_like(uu)

        def add(q, carry):
            for h in range(2):
                fill(jw, h * ROWS, blk[h, q], sig_0[h], stats[q])
            for r in range(WIDE // COLS):
                rows = slice(r * COLS, (r + 1) * COLS)
                uu[rows, r * COLS :] += dot1(jw[rows, :], jw[r * COLS :, :])
            return carry

        lax.fori_loop(0, NP, add, 0)
        turned()
        cols_in.run_all(0)
        sub = lax.broadcasted_iota(jnp.int32, (8, B), 0)
        ln = lax.broadcasted_iota(jnp.int32, (8, B), 1)
        for r in range(NB):
            rows = slice(r * B, (r + 1) * B)
            i = lax.broadcasted_iota(jnp.int32, (B, B), 0)
            j = lax.broadcasted_iota(jnp.int32, (B, B), 1)
            uu[rows, rows] += jnp.where(i == j, DAMPING, 0.0).astype(F32)

        def body(j, carry):
            factor_step(j, uu, diag, sub, ln)
            for jj in range(NB):

                @pl.when(j == jj)
                def _():
                    rows = slice(jj * B, jj * B + B)
                    low = (jj + 1) * B
                    if jj < NB - 1:
                        x = dot3(split(uu[rows, rows]), split(uu[rows, low:]), 1, 0)
                        uu[rows, low:] = x
                        xs = split(x)
                    for copy, cond in u_copies(jj):
                        pl.when(cond)(copy.start)
                    for t in range(jj + 1, NB):
                        at = t * B - low
                        left = (xs[0][:, at : at + B], xs[1][:, at : at + B])
                        right = (xs[0][:, at:], xs[1][:, at:])
                        uu[t * B : t * B + B, t * B :] -= dot3(left, right, 0, 0)

            return carry

        lax.fori_loop(0, NB, body, 0)
        for stage in (1, 2, 3):
            cols_in.run_all(stage)
        gram_first()
        cols_in.from_core()
        gram_part(0, NP)
        for jj in range(NB):
            for copy, cond in u_copies(jj):
                pl.when(cond)(copy.wait_send)
        for j in range(NB):
            uu[j * B : j * B + B, j * B : j * B + B] = diag[j * B : j * B + B, :]
        m = uu[own_cols, pl.ds(pl.multiple_of(s * ROWS, B), ROWS)]
        i = lax.broadcasted_iota(jnp.int32, (width, ROWS), 0) + p * width
        j = lax.broadcasted_iota(jnp.int32, (width, ROWS), 1) + s * ROWS
        panel[...] = jnp.where(i <= j, m, 0.0)

    @pl.when(k > 0)
    def _():
        inner = Copies()
        for t in range(BCH + 3):
            if t < BCH:
                pl.when(level > 1)(functools.partial(set_in, t))
                set_out(inner, level > 1, t)
            for stage in range(4):
                if 0 <= t - stage < BCH:
                    lead_in.run(stage, t - stage)
            if t == 1:
                turned()
                cols_in.run_all(0)
            if t == 3:
                cols_in.run_all(1)
        cols_in.run_all(2)
        lead_in.from_core()
        lead[...] = jnp.zeros_like(lead)

        def add(q, carry):
            fill(jr, 0, blk[2, q], sig_r, stats[q])
            for h in range(2):
                fill(jw, h * ROWS, blk[h, q], sig_0[h], stats[q])
            lead[...] += dot1(jw[...], jr[...])
            return carry

        groups = ((0, 1, 2), (3,), (4,), (5, 6), (7,), (8,), (9,))

        def pass_on(jj):
            arrived(u_rows(jj, c), u_recv.at[jj])
            for copy, cond in u_copies(jj):
                pl.when(cond)(copy.start)
            u_across(jj).start()

        def pass_groups(r):
            for depth in range(4):
                if 0 <= r - depth < len(groups):

                    @pl.when(level == depth + 1)
                    def _():
                        for jj in groups[r - depth]:
                            pass_on(jj)

        def substitute(r):
            for jj in groups[r]:
                arrived(u_rows(jj, 1 - c), u_core_recv.at[jj])
                rows = slice(jj * B, jj * B + B)
                done = dot3(split(uu[rows, rows]), split(lead[rows, :]), 1, 0)
                lead[rows, :] = done
                if jj < NB - 1:
                    low = (jj + 1) * B
                    lead[low:, :] -= dot3(split(uu[rows, low:]), split(done), 0, 0)

        pass_groups(0)
        lax.fori_loop(0, NP // 2, add, 0)
        pass_groups(1)
        cols_in.run_all(3)
        lax.fori_loop(NP // 2, NP, add, 0)
        pass_groups(2)
        gram_first()
        cols_in.from_core()
        gram_part(0, NP // 2)
        pass_groups(3)
        substitute(0)
        pass_groups(4)
        substitute(1)
        gram_part(NP // 2, NP)
        for depth in range(4):

            @pl.when(level == depth + 1)
            def _():
                for r in range(5 - depth, 5):
                    for jj in groups[r]:
                        pass_on(jj)

        substitute(2)
        substitute(3)
        pass_on(NB - 2)
        substitute(4)
        pass_on(NB - 1)
        substitute(5)
        substitute(6)
        panel[...] = lead[own_cols, :]
        for jj in range(NB):
            for copy, cond in u_copies(jj):
                pl.when(cond)(copy.wait_send)
            u_across(jj).wait_send()
        lead_in.drain()
        inner.drain()

    cols_in.drain()
    rows_in.drain()
    net.drain()


def far_copy(src, dst, send_sem, recv_sem, s, p):
    return pltpu.make_async_remote_copy(
        src_ref=src,
        dst_ref=dst,
        send_sem=send_sem,
        recv_sem=recv_sem,
        device_id={"samp": s, "par": p},
        device_id_type=MESH,
    )


def per_device(activations, signal):
    dma, vm = pltpu.SemaphoreType.DMA, pltpu.VMEM

    def gather_sems(pieces):
        return [dma((11, pieces)), dma((7, pieces)), dma((8, pieces)), dma((8, pieces))]

    gram, panel = pl.pallas_call(
        mega_kernel,
        name="gram_and_panels",
        out_shape=(
            jax.ShapeDtypeStruct((ROWS, WIDE), F32),
            jax.ShapeDtypeStruct((WIDE // NP, ROWS), F32),
        ),
        in_specs=[VM, VM],
        out_specs=(VM, VM),
        scratch_shapes=[
            vm((3, NP, ROWS, COLS), BF),
            vm((2, NP, ROWS, COLS), BF),
            vm((WIDE, WIDE), F32),
            vm((WIDE, ROWS), F32),
            vm((WIDE, B), F32),
            vm((ROWS, 2 * COLS), BF),
            vm((WIDE, 2 * COLS), BF),
            vm((8, COLS), F32),
            vm((NS, 8, COLS), F32),
            vm((NS, 2, ROWS), BF),
            vm((8, COLS), F32),
            vm((NP, 8, COLS), F32),
            vm((ROWS, 8), F32),
            vm((2, ROWS, 8), F32),
            vm((2, ROWS, 8), F32),
            dma((2,)),
            *gather_sems(CH), *gather_sems(BCH), *gather_sems(BCH),
            dma((4, BCH)), dma((BCH,)), dma, dma,
            dma((4, NB)), dma((NB,)), dma((NB,)), dma((NB,)),
            dma((NS,)), dma((NS,)), dma((NS,)), dma((NS,)), dma((NP,)), dma((NP,)),
        ],
        compiler_params=pltpu.CompilerParams(
            collective_id=0, has_side_effects=True, vmem_limit_bytes=60 * 2**20
        ),
    )(activations, signal.T)
    return gram, panel.T


def solution(mesh):
    return jax.shard_map(
        per_device,
        mesh=mesh,
        in_specs=(P("samp", "par"), P("samp", None)),
        out_specs=(P("samp", "par"), P("samp", "par")),
        check_vma=False,
    )
```

```python
import functools

import jax
import jax.numpy as jnp
from jax import lax
from jax.experimental import pallas as pl
from jax.experimental.pallas import tpu as pltpu
from jax.sharding import PartitionSpec as P

DAMPING = 0.5
EPSILON = 1e-05
F32 = jnp.float32
BF = jnp.bfloat16
MESH = pl.DeviceIdType.MESH
ANY = pl.BlockSpec(memory_space=pl.ANY)
VM = pl.BlockSpec(memory_space=pltpu.VMEM)

NX, NY, NZ = 4, 4, 2
NP = 8
NS = 16
ROWS = 640
COLS = 256
WIDE = 2 * ROWS
CH = 2
BCH = 2
NB = 10
B = 128


def place():
    s, p = lax.axis_index("samp"), lax.axis_index("par")
    return s, p


class Copies:
    def __init__(self):
        self.sent = []

    def send(self, src, dst, send_sem, recv_sem, s, p, cond=None):
        copy = pltpu.make_async_remote_copy(
            src_ref=src,
            dst_ref=dst,
            send_sem=send_sem,
            recv_sem=recv_sem,
            device_id={"samp": s, "par": p},
            device_id_type=MESH,
        )
        if cond is None:
            copy.start()
        else:
            pl.when(cond)(copy.start)
        self.sent.append((cond, copy))

    def drain(self):
        for cond, copy in self.sent:
            if cond is None:
                copy.wait_send()
            else:
                pl.when(cond)(copy.wait_send)


def arrived(ref, sem):
    pltpu.make_async_copy(ref, ref, sem).wait()


def split(v):
    hi = v.astype(BF)
    return hi, (v - hi.astype(F32)).astype(BF)


def dot3(a, b, ca, cb):
    dims = (((ca,), (cb,)), ((), ()))

    def one(u, v):
        return lax.dot_general(u, v, dims, preferred_element_type=F32)

    return one(a[0], b[1]) + one(a[1], b[0]) + one(a[0], b[0])


def dot1(a, b):
    return lax.dot_general(a, b, (((1,), (1,)), ((), ())), preferred_element_type=F32)


def row(v, i):
    return jnp.broadcast_to(v[i : i + 1, :], (8, B))


def lane(v, i):
    return jnp.broadcast_to(v[:, i : i + 1], (8, B))


def leaf(tiles, eye, sub):
    out = []
    for m in range(len(tiles)):
        top, unit = tiles[m], eye[m]
        cols = [[lane(tiles[i], 8 * m + b) for b in range(8)] for i in range(m, len(tiles))]
        scale, factors = None, []
        for k in range(8):
            r = lax.rsqrt(row(cols[0][k], k))
            inv = r * r
            scale = r if scale is None else jnp.where(sub == k, r, scale)
            pivots = [row(cols[0][k], b) for b in range(k + 1, 8)]
            f = [v[k] * inv for v in cols]
            for v, g in zip(cols, f):
                for b in range(k + 1, 8):
                    v[b] = v[b] - g * pivots[b - k - 1]
            if k < 7:
                below = jnp.where(sub > k, f[0], 0.0)
                top = top - below * row(top, k)
                unit = unit - below * row(unit, k)
            factors.append(f[1:])
        for n, i in enumerate(range(m + 1, len(tiles))):
            da = functools.reduce(jnp.add, [factors[k][n] * row(top, k) for k in range(8)])
            du = functools.reduce(jnp.add, [factors[k][n] * row(unit, k) for k in range(8)])
            tiles[i] = tiles[i] - da
            eye[i] = eye[i] - du
        out.append((unit * scale, top * scale))
    return out


def fill(dst, base, act, sig_cols, stat):
    a = act.astype(F32)
    for o in range(2):
        v = sig_cols[:, o : o + 1] * a
        v = (v - stat[2 * o : 2 * o + 1]) * stat[2 * o + 1 : 2 * o + 2]
        dst[base : base + ROWS, o * COLS : (o + 1) * COLS] = v.astype(BF)


def cols_of(rows):
    return jnp.transpose(jnp.concatenate([rows.astype(F32), jnp.zeros((6, ROWS), F32)], axis=0))


def greet(s, p):
    c, k = lax.rem(s, 2), s // 2
    barrier = pltpu.get_barrier_semaphore()

    def signal(to_s, to_p):
        pl.semaphore_signal(
            barrier, inc=1, device_id={"samp": to_s, "par": to_p}, device_id_type=MESH
        )

    for i in range(1, NS):
        signal(lax.rem(s + i, NS), p)
    for i in range(1, NP):
        signal(s, lax.rem(p + i, NP))

    @pl.when(k != p)
    def _():
        signal(2 * p + c, k)

    pl.semaphore_wait(barrier, NS + NP - 2 + jnp.where(k == p, 0, 1))


class Place:
    def __init__(self):
        s, p = lax.axis_index("samp"), lax.axis_index("par")
        self.s, self.p = s, p
        self.c, self.k = lax.rem(s, 2), s // 2
        self.x, self.zh = lax.rem(self.k, NX), self.k // NX
        self.y, self.zl = p // NZ, lax.rem(p, NZ)
        self.other = s + 1 - 2 * self.c
    def samp_of(self, zz, xx):
        return 2 * (zz * NX + xx) + self.c

    def tree(self):
        x, zh, c = self.x, self.zh, self.c
        root = jnp.where(zh == 0, 0, c)
        turn = lax.rem(x - root + NX, NX)
        side = jnp.where(c == zh, turn == 1, turn == 3)
        return [
            (self.samp_of(zh, lax.rem(root + 1, NX)), turn == 0),
            (self.samp_of(zh, lax.rem(root + 3, NX)), turn == 0),
            (self.samp_of(1, x), jnp.logical_and(zh == 0, x == c)),
            (self.samp_of(zh, lax.rem(root + 2, NX)), side),
        ]

    def level(self):
        root = jnp.where(self.zh == 0, 0, self.c)
        turn = lax.rem(self.x - root + NX, NX)
        return jnp.where(self.zh == 0, 0, 1 + self.c) + jnp.where(turn == 2, 2, jnp.where(turn == 0, 0, 1))


class Gather:
    def __init__(self, here, buf, index, ring, pair, where, pieces, sems, core=True, by_ring=False, busy=None):
        self.here, self.buf, self.index = here, buf, index
        self.ring, self.pair, self.where = ring, pair, where
        self.up, self.down = lax.rem(ring + 1, 4), lax.rem(ring + 3, 4)
        self.far, self.lo = lax.rem(ring + 2, 4), 1 - pair
        self.ahead = jnp.where(here.c == 0, self.up, self.down)
        self.behind = jnp.where(here.c == 0, self.down, self.up)
        self.pieces, self.step, self.sems = pieces, ROWS // pieces, sems
        self.core, self.by_ring, self.busy = core, by_ring, busy

    def part(self, r, q, t, other=False):
        slot, _, _ = self.where(r, q)
        index = 1 - self.index if other else self.index
        return self.buf.at[index, slot, pl.ds(t * self.step, self.step), :]

    def wait(self, r, q, t, i):
        return ("wait", self.part(r, q, t), self.sems[1].at[i, t])

    def send(self, r, q, t, i, to_r, to_q):
        _, to_s, to_p = self.where(to_r, to_q)
        ref = self.part(r, q, t)
        copy = far_copy(ref, ref, self.sems[0].at[i, t], self.sems[1].at[i, t], to_s, to_p)
        return ("send", copy, None)

    def relay(self, *args):
        kind, copy, _ = self.send(*args)
        return (kind, copy, None if self.busy is None else jnp.logical_not(self.busy))

    def direct(self, t):
        if self.busy is None:
            return []
        r, q, c = self.ring, self.pair, self.here.c
        end = jnp.where(r == 3, 1, 3)
        side = jnp.where(c == 0, r == 3, r == 1)
        ref = self.part(r, q, t)
        found = []
        for n, (i, to, cond) in enumerate((
            (3, 1, jnp.logical_and(r == 0, q == 1)),
            (4, 3, jnp.logical_and(r == 0, q == 1)),
            (5, end, jnp.logical_and(side, q == 0)),
            (6, end, jnp.logical_and(side, q == 1)),
        )):
            _, to_s, to_p = self.where(to, 0)
            copy = far_copy(ref, ref, self.sems[0].at[7 + n, t], self.sems[1].at[i, t], to_s, to_p)
            found.append(("send", copy, cond))
        return found

    def across(self, r, q, t, i):
        ref, here = self.part(r, q, t), self.here
        copy = far_copy(ref, ref, self.sems[2].at[i, t], self.sems[3].at[i, t], here.other, here.p)
        return ("send", copy, None if self.core is True else self.core)

    def events(self, stage, t):
        r, q, up, down, far, lo = self.ring, self.pair, self.up, self.down, self.far, self.lo
        if stage == 0:
            return [
                self.send(r, q, t, 1, up, q),
                self.send(r, q, t, 2, down, q),
                self.send(r, q, t, 0, r, lo),
                self.across(r, q, t, 0),
                *self.direct(t),
            ]
        if stage == 1:
            return [
                self.wait(r, lo, t, 0),
                self.relay(r, lo, t, 3, up, q),
                self.relay(r, lo, t, 4, down, q),
                self.across(r, lo, t, 1),
                self.wait(down, q, t, 1),
                self.wait(up, q, t, 2),
                self.relay(self.behind, q, t, 5, self.ahead, q),
                self.across(down, q, t, 2),
                self.across(up, q, t, 3),
            ]
        if stage == 2:
            hand_on = [self.relay(far, q, t, 6, r, lo)]
            relayed = [self.relay(self.behind, lo, t, 6, self.ahead, q)]
            return [
                self.wait(far, q, t, 5),
                *([] if self.by_ring else hand_on),
                self.across(far, q, t, 4),
                self.wait(down, lo, t, 3),
                self.wait(up, lo, t, 4),
                *(relayed if self.by_ring else []),
                self.across(down, lo, t, 5),
                self.across(up, lo, t, 6),
            ]
        return [self.wait(far, lo, t, 6), self.across(far, lo, t, 7)]

    def run(self, stage, t):
        for event in self.events(stage, t):
            if event[0] == "wait":
                arrived(*event[1:])
            elif event[2] is None:
                event[1].start()
            else:
                pl.when(event[2])(event[1].start)

    def run_all(self, stage):
        for t in range(self.pieces):
            self.run(stage, t)

    def from_core(self):
        r, q, up, down, far, lo = self.ring, self.pair, self.up, self.down, self.far, self.lo
        order = [(r, q), (r, lo), (down, q), (up, q), (far, q), (down, lo), (up, lo), (far, lo)]
        for t in range(self.pieces):
            for i, (a, b) in enumerate(order):
                arrived(self.part(a, b, t, other=True), self.sems[3].at[i, t])

    def drain(self):
        for stage in range(4):
            for t in range(self.pieces):
                for kind, copy, cond in self.events(stage, t):
                    if kind == "send":
                        if cond is None:
                            copy.wait_send()
                        else:
                            pl.when(cond)(copy.wait_send)


def own_sums(act, sig):
    def add(i, sums):
        rows = pl.ds(pl.multiple_of(i * 80, 80), 80)
        a = act[rows, :].astype(F32)
        g = sig[rows, :]
        new = []
        for o in range(2):
            v = g[:, o : o + 1] * a
            new.append(sums[2 * o] + jnp.sum(v.reshape(10, 8, COLS), axis=0))
            new.append(sums[2 * o + 1] + jnp.sum((v * v).reshape(10, 8, COLS), axis=0))
        return tuple(new)

    zero = jnp.zeros((8, COLS), F32)
    sums = lax.fori_loop(0, ROWS // 80, add, (zero,) * 4)
    return jnp.concatenate(
        [jnp.sum(v, axis=0, keepdims=True) for v in sums] + [jnp.zeros((4, COLS), F32)], axis=0
    )


def statistics(total):
    count, width = float(NS * ROWS), float(2 * COLS * NP)
    rows = []
    for o in range(2):
        average = total[2 * o : 2 * o + 1] / count
        second = total[2 * o + 1 : 2 * o + 2] / count
        rows += [average, 1.0 / jnp.sqrt(width * (second - average * average + EPSILON))]
    return jnp.concatenate(rows + [jnp.zeros((4, COLS), F32)], axis=0)


def factor_step(j, uu, diag, sub, ln):
    j0 = pl.multiple_of(j * B, B)
    here = pl.ds(j0, B)
    tiles = [uu[pl.ds(pl.multiple_of(j0 + 8 * i, 8), 8), here] for i in range(B // 8)]
    eye = [jnp.where(ln == sub + 8 * i, 1.0, 0.0).astype(F32) for i in range(B // 8)]
    for i, (w, u) in enumerate(leaf(tiles, eye, sub)):
        rows = pl.ds(pl.multiple_of(j0 + 8 * i, 8), 8)
        uu[rows, here] = w
        diag[rows, :] = u


def mega_kernel(
    act, sig, gram, panel,
    blk, ac, uu, lead, diag, jr, jw, mom, moms, sigs, stat, stats, sig_r, sig_c, sig_0,
    own_sem, a_two_send, a_two_recv, a_core_send, a_core_recv,
    b_two_send, b_two_recv, b_core_send, b_core_recv,
    c_two_send, c_two_recv, c_core_send, c_core_recv, one_send, one_recv,
    t_send, t_recv, u_send, u_recv, u_core_send, u_core_recv,
    mom_send, mom_recv, sig_send, sig_recv, stat_send, stat_recv,
):
    here = Place()
    s, p, c, k = here.s, here.p, here.c, here.k
    own_slot = jnp.where(k == 0, c, 2)
    net = Copies()
    first = pltpu.make_async_copy(act, blk.at[own_slot, p], own_sem.at[0])
    first.start()
    turn = pltpu.make_async_copy(act, ac.at[c, k], own_sem.at[1])

    @pl.when(k == p)
    def _():
        turn.start()

    sigs[s] = sig[...]
    sig_r[...] = cols_of(sig[...])
    greet(s, p)
    first.wait()

    def on_par(r, q):
        return r * NZ + q, s, r * NZ + q

    def on_samp(r, q):
        return q * NX + r, here.samp_of(q, r), p

    rows_in = Gather(
        here, blk, own_slot, here.y, here.zl, on_par, CH,
        (a_two_send, a_two_recv, a_core_send, a_core_recv), core=k == 0,
    )
    lead_in = Gather(
        here, blk, c, here.y, here.zl, on_par, BCH,
        (b_two_send, b_two_recv, b_core_send, b_core_recv),
    )
    cols_in = Gather(
        here, ac, c, here.x, here.zh, on_samp, BCH,
        (c_two_send, c_two_recv, c_core_send, c_core_recv), by_ring=True, busy=k == 0,
    )

    def turned():
        @pl.when(k == p)
        def _():
            turn.wait()

        @pl.when(k != p)
        def _():
            arrived(ac.at[c, k], t_recv)

    level = here.level()

    def set_out(copies, when, only):
        for n in range(BCH) if only is None else [only]:
            ref = lead_in.part(here.y, here.zl, n)
            for i, (to, cond) in enumerate(here.tree()):
                copies.send(ref, ref, one_send.at[i, n], one_recv.at[n], to, p, jnp.logical_and(when, cond))

    def set_in(n):
        arrived(lead_in.part(here.y, here.zl, n), one_recv.at[n])

    for t in range(CH + 3):
        for stage in range(4):
            if 0 <= t - stage < CH:
                rows_in.run(stage, t - stage)
        if t == 0:
            set_out(net, k == 0, None)
            wanted = jnp.logical_or(k == 0, k == p)
            for i in range(1, NS):
                to = lax.rem(s + i, NS)
                net.send(sig, sigs.at[s], sig_send.at[i], sig_recv.at[s], to, p, wanted)
            mom[...] = own_sums(act, sig_r)
            for i in range(1, NS):
                net.send(mom, moms.at[s], mom_send.at[i], mom_recv.at[s], lax.rem(s + i, NS), p)
            moms[s] = mom[...]
        if t == 3:
            for i in range(1, NS):
                j = lax.rem(s + i, NS)
                arrived(moms.at[j], mom_recv.at[j])
            total = moms[0]
            for j in range(1, NS):
                total = total + moms[j]
            stat[...] = statistics(total)
            for i in range(1, NP):
                net.send(stat, stats.at[p], stat_send.at[i], stat_recv.at[p], s, lax.rem(p + i, NP))
            stats[p] = stat[...]

    net.send(act, ac.at[c, p], t_send, t_recv, 2 * p + c, k, k != p)

    @pl.when(level == 1)
    def _():
        for n in range(BCH):
            set_in(n)

    set_out(net, level == 1, None)
    for h in range(2):
        for j, cond in ((h, s != h), (2 * p + h, jnp.logical_and(p > 0, s != 2 * p + h))):
            pl.when(cond)(functools.partial(arrived, sigs.at[j], sig_recv.at[j]))
    for h in range(2):
        sig_c[h] = cols_of(sigs[2 * p + h])
        sig_0[h] = cols_of(sigs[h])
    for i in range(1, NP):
        j = lax.rem(p + i, NP)
        arrived(stats.at[j], stat_recv.at[j])

    def gram_part(start, stop):
        def add(q, carry):
            fill(jr, 0, blk[own_slot, q], sig_r, stats[q])
            for h in range(2):
                fill(jw, h * ROWS, ac[h, q], sig_c[h], stats[q])
            gram[...] += dot1(jr[...], jw[...])
            return carry

        lax.fori_loop(start, stop, add, 0)

    def gram_first():
        i = lax.broadcasted_iota(jnp.int32, (ROWS, WIDE), 0) + s * ROWS
        j = lax.broadcasted_iota(jnp.int32, (ROWS, WIDE), 1) + p * WIDE
        gram[...] = jnp.where(i == j, DAMPING, 0.0).astype(F32)

    def u_rows(jj, half):
        return uu.at[pl.ds(jj * B + half * (B // 2), B // 2), jj * B :]

    def u_copies(jj):
        ref = u_rows(jj, c)
        return [
            (far_copy(ref, ref, u_send.at[i, jj], u_recv.at[jj], to, p), cond)
            for i, (to, cond) in enumerate(here.tree())
        ]

    def u_across(jj):
        ref = u_rows(jj, c)
        return far_copy(ref, ref, u_core_send.at[jj], u_core_recv.at[jj], here.other, p)

    width = WIDE // NP
    own_cols = pl.ds(pl.multiple_of(p * width, 8), width)

    @pl.when(k == 0)
    def _():
        rows_in.from_core()
        uu[...] = jnp.zeros_like(uu)

        def add(q, carry):
            for h in range(2):
                fill(jw, h * ROWS, blk[h, q], sig_0[h], stats[q])
            for r in range(WIDE // COLS):
                rows = slice(r * COLS, (r + 1) * COLS)
                uu[rows, r * COLS :] += dot1(jw[rows, :], jw[r * COLS :, :])
            return carry

        lax.fori_loop(0, NP, add, 0)
        turned()
        cols_in.run_all(0)
        sub = lax.broadcasted_iota(jnp.int32, (8, B), 0)
        ln = lax.broadcasted_iota(jnp.int32, (8, B), 1)
        for r in range(NB):
            rows = slice(r * B, (r + 1) * B)
            i = lax.broadcasted_iota(jnp.int32, (B, B), 0)
            j = lax.broadcasted_iota(jnp.int32, (B, B), 1)
            uu[rows, rows] += jnp.where(i == j, DAMPING, 0.0).astype(F32)

        def body(j, carry):
            factor_step(j, uu, diag, sub, ln)
            for jj in range(NB):

                @pl.when(j == jj)
                def _():
                    rows = slice(jj * B, jj * B + B)
                    low = (jj + 1) * B
                    if jj < NB - 1:
                        x = dot3(split(uu[rows, rows]), split(uu[rows, low:]), 1, 0)
                        uu[rows, low:] = x
                        xs = split(x)
                    for copy, cond in u_copies(jj):
                        pl.when(cond)(copy.start)
                    for t in range(jj + 1, NB):
                        at = t * B - low
                        left = (xs[0][:, at : at + B], xs[1][:, at : at + B])
                        right = (xs[0][:, at:], xs[1][:, at:])
                        uu[t * B : t * B + B, t * B :] -= dot3(left, right, 0, 0)

            return carry

        lax.fori_loop(0, NB, body, 0)
        for stage in (1, 2, 3):
            cols_in.run_all(stage)
        gram_first()
        cols_in.from_core()
        gram_part(0, NP)
        for jj in range(NB):
            for copy, cond in u_copies(jj):
                pl.when(cond)(copy.wait_send)
        for j in range(NB):
            uu[j * B : j * B + B, j * B : j * B + B] = diag[j * B : j * B + B, :]
        m = uu[own_cols, pl.ds(pl.multiple_of(s * ROWS, B), ROWS)]
        i = lax.broadcasted_iota(jnp.int32, (width, ROWS), 0) + p * width
        j = lax.broadcasted_iota(jnp.int32, (width, ROWS), 1) + s * ROWS
        panel[...] = jnp.where(i <= j, m, 0.0)

    @pl.when(k > 0)
    def _():
        inner = Copies()
        for t in range(BCH + 3):
            if t < BCH:
                pl.when(level > 1)(functools.partial(set_in, t))
                set_out(inner, level > 1, t)
            for stage in range(4):
                if 0 <= t - stage < BCH:
                    lead_in.run(stage, t - stage)
            if t == 1:
                turned()
                cols_in.run_all(0)
            if t == 3:
                cols_in.run_all(1)
        cols_in.run_all(2)
        lead_in.from_core()
        lead[...] = jnp.zeros_like(lead)

        def add(q, carry):
            fill(jr, 0, blk[2, q], sig_r, stats[q])
            for h in range(2):
                fill(jw, h * ROWS, blk[h, q], sig_0[h], stats[q])
            lead[...] += dot1(jw[...], jr[...])
            return carry

        groups = ((0, 1, 2), (3,), (4,), (5, 6), (7,), (8,), (9,))

        def pass_on(jj):
            arrived(u_rows(jj, c), u_recv.at[jj])
            for copy, cond in u_copies(jj):
                pl.when(cond)(copy.start)
            u_across(jj).start()

        def pass_groups(r):
            for depth in range(4):
                if 0 <= r - depth < len(groups):

                    @pl.when(level == depth + 1)
                    def _():
                        for jj in groups[r - depth]:
                            pass_on(jj)

        def substitute(r):
            for jj in groups[r]:
                arrived(u_rows(jj, 1 - c), u_core_recv.at[jj])
                rows = slice(jj * B, jj * B + B)
                done = dot3(split(uu[rows, rows]), split(lead[rows, :]), 1, 0)
                lead[rows, :] = done
                if jj < NB - 1:
                    low = (jj + 1) * B
                    lead[low:, :] -= dot3(split(uu[rows, low:]), split(done), 0, 0)

        pass_groups(0)
        lax.fori_loop(0, NP // 2, add, 0)
        pass_groups(1)
        cols_in.run_all(3)
        lax.fori_loop(NP // 2, NP, add, 0)
        pass_groups(2)
        gram_first()
        cols_in.from_core()
        gram_part(0, NP // 2)
        pass_groups(3)
        substitute(0)
        pass_groups(4)
        substitute(1)
        gram_part(NP // 2, NP)
        for depth in range(4):

            @pl.when(level == depth + 1)
            def _():
                for r in range(5 - depth, 5):
                    for jj in groups[r]:
                        pass_on(jj)

        substitute(2)
        substitute(3)
        pass_on(NB - 2)
        substitute(4)
        pass_on(NB - 1)
        substitute(5)
        substitute(6)
        panel[...] = lead[own_cols, :]
        for jj in range(NB):
            for copy, cond in u_copies(jj):
                pl.when(cond)(copy.wait_send)
            u_across(jj).wait_send()
        lead_in.drain()
        inner.drain()

    cols_in.drain()
    rows_in.drain()
    net.drain()


def far_copy(src, dst, send_sem, recv_sem, s, p):
    return pltpu.make_async_remote_copy(
        src_ref=src,
        dst_ref=dst,
        send_sem=send_sem,
        recv_sem=recv_sem,
        device_id={"samp": s, "par": p},
        device_id_type=MESH,
    )


def per_device(activations, signal):
    dma, vm = pltpu.SemaphoreType.DMA, pltpu.VMEM

    def gather_sems(pieces):
        return [dma((11, pieces)), dma((7, pieces)), dma((8, pieces)), dma((8, pieces))]

    gram, panel = pl.pallas_call(
        mega_kernel,
        name="gram_and_panels",
        out_shape=(
            jax.ShapeDtypeStruct((ROWS, WIDE), F32),
            jax.ShapeDtypeStruct((WIDE // NP, ROWS), F32),
        ),
        in_specs=[VM, VM],
        out_specs=(VM, VM),
        scratch_shapes=[
            vm((3, NP, ROWS, COLS), BF),
            vm((2, NP, ROWS, COLS), BF),
            vm((WIDE, WIDE), F32),
            vm((WIDE, ROWS), F32),
            vm((WIDE, B), F32),
            vm((ROWS, 2 * COLS), BF),
            vm((WIDE, 2 * COLS), BF),
            vm((8, COLS), F32),
            vm((NS, 8, COLS), F32),
            vm((NS, 2, ROWS), BF),
            vm((8, COLS), F32),
            vm((NP, 8, COLS), F32),
            vm((ROWS, 8), F32),
            vm((2, ROWS, 8), F32),
            vm((2, ROWS, 8), F32),
            dma((2,)),
            *gather_sems(CH), *gather_sems(BCH), *gather_sems(BCH),
            dma((4, BCH)), dma((BCH,)), dma, dma,
            dma((4, NB)), dma((NB,)), dma((NB,)), dma((NB,)),
            dma((NS,)), dma((NS,)), dma((NS,)), dma((NS,)), dma((NP,)), dma((NP,)),
        ],
        compiler_params=pltpu.CompilerParams(
            collective_id=0, has_side_effects=True, vmem_limit_bytes=48 * 2**20
        ),
    )(activations, signal.T)
    return gram, panel.T


def solution(mesh):
    return jax.shard_map(
        per_device,
        mesh=mesh,
        in_specs=(P("samp", "par"), P("samp", None)),
        out_specs=(P("samp", "par"), P("samp", "par")),
        check_vma=False,
    )
```
